32 devices in a mesh: row: 8 (over y, x, core), col: 4 (over z).
Axes of the slice: x: 2, y: 2, z: 4, core: 2. Of those that a mesh axis runs over, the one named last changes fastest.
Arguments:
- covariance: float32 [4096, 2, 2048], P('row', None, 'col'), may hold values from 0 to 1.1, as said below
- diag_inverse: float32 [512, 512], replicated, as said below
Outputs:
- panels: float32 [4096, 1024], P('row', 'col')
- trailing: float32 [4096, 2, 2048], P('row', None, 'col')
The draws below stay inside these ranges and needn't reach their ends.
Inputs may be any that keep to these rules, and one draw needn't show every extreme that they name: `covariance`: K is symmetric and positive definite, its smallest eigenvalue 0.1 or more. `diag_inverse`: the inverse of the lower Cholesky factor of K[0:512, 0:512].
All inputs are finite; a program needn't handle non-finite values.
Results may differ from the reference program's by a relative error of at most 0.0003.
Values sent between devices are 32-bit elements; how exact they have to be, the bound alone decides.
No kernel may reach another device: no remote copies, remote signals or barrier semaphores. Data moves between devices by JAX's collectives and lax.ppermute only.
A program may use at most 128 MiB of HBM per device.

```python
import jax
import jax.numpy as jnp
from jax import lax

TILE = 512
FEAT = 64
TILES = 8
ORDER = 4096
CYCLES = 2
N_COL = 4


highest = lax.Precision.HIGHEST


length_scale = 1.5


nugget = 0.1


dist_floor = 0.01


def matern(left_points, right_points):
    left_sq = jnp.sum(left_points * left_points, axis=0)
    right_sq = jnp.sum(right_points * right_points, axis=0)
    products = lax.dot_general(left_points, right_points, (((0,), (0,)), ((), ())), precision=highest, preferred_element_type=jnp.float32)
    dist_sq = jnp.maximum(left_sq[:, None] + right_sq[None, :] - 2.0 * products, dist_floor)
    scaled = jnp.sqrt(3.0 * dist_sq) / length_scale
    return (1.0 + scaled) * jnp.exp(-scaled)


def kernel_tile(row_points, col_points, row_start, col_start):
    tile_shape = (row_points.shape[1], col_points.shape[1])
    row_ids = row_start + lax.broadcasted_iota(jnp.int32, tile_shape, 0)
    col_ids = col_start + lax.broadcasted_iota(jnp.int32, tile_shape, 1)
    return matern(row_points, col_points) + jnp.where(row_ids == col_ids, nugget, 0.0)


def shared_points(key):
    base_key = jax.random.fold_in(key, 4242)
    spread = FEAT ** (-0.5)
    values = jax.random.normal(jax.random.fold_in(base_key, 3), (FEAT, ORDER), jnp.float32)
    return jnp.clip(values * spread, -4.0 * spread, 4.0 * spread)


def draw_covariance(key, part):
    points = shared_points(key)

    def one_column(column):
        col_points = lax.dynamic_slice_in_dim(points, column * TILE, TILE, 1)
        return kernel_tile(points, col_points, jnp.int32(0), column * TILE)
    stacked = lax.map(one_column, jnp.arange(TILES, dtype=jnp.int32))
    return stacked.reshape(CYCLES, N_COL, ORDER, TILE).transpose(2, 0, 1, 3).reshape(ORDER, CYCLES, N_COL * TILE)


def draw_diag_inverse(key, part):
    lead_points = shared_points(key)[:, :TILE]
    identity = jnp.eye(TILE, dtype=jnp.float32)
    block_lead = kernel_tile(lead_points, lead_points, jnp.int32(0), jnp.int32(0))
    factor = jnp.linalg.cholesky(block_lead)
    return jax.scipy.linalg.solve_triangular(factor, identity, lower=True)


def setup_inputs(seed: int = 0) -> dict:
    key_of = jax.random.split(jax.random.key(seed), 3)
    return {
        "covariance": draw_covariance(jax.random.fold_in(key_of[2], 71), 0),
        "diag_inverse": draw_diag_inverse(jax.random.fold_in(key_of[2], 71), 0),
    }


highest = lax.Precision.HIGHEST

def outer_product(left, right):
    return lax.dot_general(left, right, (((1,), (1,)), ((), ())), precision=highest, preferred_element_type=left.dtype)

def reference(covariance, diag_inverse):
    order_size = covariance.shape[0]

    def column_block(column):
        start = (jnp.int32(0), (column // N_COL).astype(jnp.int32), (column % N_COL * TILE).astype(jnp.int32))
        piece = lax.dynamic_slice(covariance, start, (order_size, 1, TILE))
        return piece.reshape(order_size, TILE)
    panel_one = outer_product(column_block(jnp.int32(0)), diag_inverse)
    second = column_block(jnp.int32(1)) - outer_product(panel_one, panel_one[TILE:2 * TILE])
    factor = jnp.linalg.cholesky(second[TILE:2 * TILE])
    solved = jax.scipy.linalg.solve_triangular(factor, second.T, lower=True).T
    row_ids = lax.broadcasted_iota(jnp.int32, (order_size, TILE), 0)
    panel_two = jnp.where(row_ids >= TILE, solved, 0.0)

    def one_column(column):
        top_row = (column * TILE).astype(jnp.int32)
        current = column_block(column)
        current = current - outer_product(panel_one, lax.dynamic_slice_in_dim(panel_one, top_row, TILE, 0))
        current = current - outer_product(panel_two, lax.dynamic_slice_in_dim(panel_two, top_row, TILE, 0))
        keep_mask = (row_ids >= top_row) & (column >= 2)
        return jnp.where(keep_mask, current, 0.0)
    stacked = lax.map(one_column, jnp.arange(TILES, dtype=jnp.int32))
    trailing = stacked.reshape(CYCLES, N_COL, order_size, TILE).transpose(2, 0, 1, 3).reshape(order_size, CYCLES, N_COL * TILE)
    return (jnp.concatenate([panel_one, panel_two], axis=1), trailing)
```

```python
import functools

import jax
import jax.numpy as jnp
from jax import lax
from jax.experimental import pallas as pl
from jax.experimental.pallas import tpu as pltpu
from jax.sharding import PartitionSpec as P

HIGHEST = lax.Precision.HIGHEST
AXES = ("row", "col")
SUB = 8
BLOCK = 128


def dot(left, right, lhs_dim, rhs_dim):
    return lax.dot_general(
        left,
        right,
        (((lhs_dim,), (rhs_dim,)), ((), ())),
        precision=HIGHEST,
        preferred_element_type=jnp.float32,
    )


def nn(left, right):
    return dot(left, right, 1, 0)


def nt(left, right):
    return dot(left, right, 1, 1)


def tn(left, right):
    return dot(left, right, 0, 0)


def factor_block(work, aug):
    size = work.shape[0]
    groups = size // SUB
    rows = lax.broadcasted_iota(jnp.int32, (SUB, size), 0)
    lanes = lax.broadcasted_iota(jnp.int32, (SUB, size), 1)
    for t in range(groups):
        aug[t * SUB : (t + 1) * SUB, :] = jnp.where(lanes == rows + t * SUB, 1.0, 0.0)

    def lane(value, index):
        return jnp.broadcast_to(value[:, index : index + 1], (SUB, size))

    def row(value, index):
        return jnp.broadcast_to(value[index : index + 1, :], (SUB, size))

    for s in range(groups):
        here = slice(s * SUB, (s + 1) * SUB)
        own, own_aug = work[here, :], aug[here, :]
        columns = [lane(own, s * SUB + b) for b in range(SUB)]
        small = [[row(columns[b], a) if a >= b else None for b in range(SUB)] for a in range(SUB)]
        upper = [row(own, i) for i in range(SUB)]
        inverse = [row(own_aug, i) for i in range(SUB)]
        low = [[None] * SUB for _ in range(SUB)]
        scale = []
        for i in range(SUB):
            scale.append(lax.rsqrt(small[i][i]))
            for a in range(i + 1, SUB):
                low[a][i] = small[a][i] * scale[i]
            for b in range(i + 1, SUB):
                for a in range(b, SUB):
                    small[a][b] = small[a][b] - low[a][i] * low[b][i]
            upper[i] = upper[i] * scale[i]
            inverse[i] = inverse[i] * scale[i]
            for b in range(i + 1, SUB):
                upper[b] = upper[b] - upper[i] * low[b][i]
                inverse[b] = inverse[b] - inverse[i] * low[b][i]
        for t in range(s + 1, groups):
            there = slice(t * SUB, (t + 1) * SUB)
            current, current_aug = work[there, :], aug[there, :]
            part = [lane(current, s * SUB + b) for b in range(SUB)]
            for i in range(SUB):
                part[i] = part[i] * scale[i]
                for b in range(i + 1, SUB):
                    part[b] = part[b] - part[i] * low[b][i]
                current = current - part[i] * upper[i]
                current_aug = current_aug - part[i] * inverse[i]
            work[there, :] = current
            aug[there, :] = current_aug
        packed_inverse, packed_upper = inverse[0], upper[0]
        for i in range(1, SUB):
            packed_inverse = jnp.where(rows == i, inverse[i], packed_inverse)
            packed_upper = jnp.where(rows == i, upper[i], packed_upper)
        aug[here, :] = jnp.where(lanes <= rows + s * SUB, packed_inverse, packed_upper)


def lower_part(packed):
    rows = lax.broadcasted_iota(jnp.int32, packed.shape, 0)
    lanes = lax.broadcasted_iota(jnp.int32, packed.shape, 1)
    return jnp.where(lanes <= rows, packed, 0.0)


def factor_kernel(flag_ref, block_ref, out_ref, work, diag, aug):
    size = block_ref.shape[0]
    blocks = size // BLOCK

    @pl.when(flag_ref[0] == 1)
    def _():
        work[...] = block_ref[...]
        for k in range(blocks):
            here, rest = slice(k * BLOCK, (k + 1) * BLOCK), slice((k + 1) * BLOCK, size)
            diag[...] = work[here, here]
            factor_block(diag, aug)
            packed = aug[...]
            inverse = lower_part(packed)
            out_ref[here, here] = packed
            if k:
                coupling = jnp.zeros((BLOCK, k * BLOCK), jnp.float32)
                for j in range(k):
                    below = slice(j * BLOCK, (j + 1) * BLOCK)
                    width = slice(0, (j + 1) * BLOCK)
                    rows_j = out_ref[below, width]
                    if j == 0:
                        rows_j = lower_part(rows_j)
                    else:
                        row_ids = lax.broadcasted_iota(jnp.int32, rows_j.shape, 0) + j * BLOCK
                        lane_ids = lax.broadcasted_iota(jnp.int32, rows_j.shape, 1)
                        rows_j = jnp.where(lane_ids <= row_ids, rows_j, 0.0)
                    term = tn(out_ref[below, here], rows_j)
                    if (j + 1) < k:
                        term = jnp.concatenate(
                            [term, jnp.zeros((BLOCK, (k - j - 1) * BLOCK), jnp.float32)], axis=1
                        )
                    coupling = coupling + term
                out_ref[here, : k * BLOCK] = -nn(inverse, coupling)
            if k + 1 < blocks:
                upper = nn(inverse, work[here, rest])
                out_ref[here, rest] = upper
                for j in range(k + 1, blocks):
                    below = slice(j * BLOCK, (j + 1) * BLOCK)
                    tail = slice(j * BLOCK, size)
                    left = upper[:, (j - k - 1) * BLOCK : (j - k) * BLOCK]
                    right = upper[:, (j - k - 1) * BLOCK :]
                    work[below, tail] = work[below, tail] - tn(left, right)


def factor(flag, block):
    size = block.shape[0]
    return pl.pallas_call(
        factor_kernel,
        out_shape=jax.ShapeDtypeStruct((size, size), jnp.float32),
        in_specs=[
            pl.BlockSpec(memory_space=pltpu.SMEM),
            pl.BlockSpec(memory_space=pltpu.VMEM),
        ],
        out_specs=pl.BlockSpec(memory_space=pltpu.VMEM),
        scratch_shapes=[
            pltpu.VMEM((size, size), jnp.float32),
            pltpu.VMEM((BLOCK, BLOCK), jnp.float32),
            pltpu.VMEM((BLOCK, BLOCK), jnp.float32),
        ],
        name="factor",
    )(flag, block)


def local(covariance, diag_inverse, rows, cols):
    tile = covariance.shape[0]
    cycles = covariance.shape[1]
    half = tile // 2
    chips = rows // 2
    r, c = lax.axis_index("row"), lax.axis_index("col")
    chip, core = r // 2, r % 2
    slots = [covariance[:, m, :] for m in range(cycles)]

    def send(value, pairs):
        flat = [(a * cols + b, x * cols + y) for (a, b), (x, y) in pairs]
        return lax.ppermute(value, AXES, flat) if flat else jnp.zeros_like(value)

    def column_of(t, column):
        return (t + (1 if column < 2 else 0)) * cols + column

    def held(t):
        later = slots[t + 1] if t + 1 < cycles else slots[t]
        return jnp.where(c < 2, later, slots[t])

    first_column = jnp.where(c < 2, 1, 0)

    swap_pairs = [((1, b), (0, b)) for b in range(cols)]
    swapped = send(
        jnp.where(core == 0, slots[0], held(0)), swap_pairs + [((0, 1), (1, 1))]
    )
    others = [swapped] + [send(held(t), swap_pairs[2:]) for t in range(1, cycles)]

    bits = []
    while (1 << len(bits)) < chips:
        bits.append(1 << len(bits))

    def spread(pieces, wanted):
        orders = (bits, bits[::-1])
        current = list(pieces)
        for step in range(len(bits)):
            for which, order in enumerate(orders):
                used = sum(order[:step])
                bit, later = order[step], sum(order[step + 1 :])
                pairs = []
                for column in range(cols):
                    for q in range(chips):
                        target = q | bit
                        if q & ~used or target >= chips:
                            continue
                        reach = {target | extra for extra in range(chips) if not extra & ~later}
                        if reach & wanted(column):
                            pairs.append(((2 * q, column), (2 * target, column)))
                got = send(current[which], pairs)
                current[which] = jnp.where((chip & bit) != 0, got, current[which])
        return current

    core_pairs = [((2 * q, b), (2 * q + 1, b)) for q in range(chips) for b in range(cols)]

    col_first, col_second = [], []
    for t in range(cycles):

        def wanted(column, t=t):
            if column < 2 and t + 1 >= cycles:
                return set()
            return {q for q in range(chips) if 2 * q + 1 >= column_of(t, column)}

        both = [
            jnp.concatenate([held(t)[part], others[t][part]], axis=0)
            for part in (slice(0, half), slice(half, tile))
        ]
        both = spread(both, wanted)
        pairs = [
            pair for pair in core_pairs if pair[0][0] // 2 in wanted(pair[0][1]) and pair[0][0] > 0
        ]
        whole = jnp.concatenate(both, axis=0)
        whole = jnp.where(core == 0, whole, send(whole, pairs))
        col_first.append(jnp.concatenate([whole[:half], whole[tile : tile + half]], axis=0))
        col_second.append(jnp.concatenate([whole[half:tile], whole[tile + half :]], axis=0))

    corner = slots[0]
    for b in range(cols):
        if b != 1:
            corner = jnp.where(c == b, send(slots[0], [((0, 1), (0, b))]), corner)
    everyone = set(range(chips))
    corner = jnp.concatenate(spread([corner[:half], corner[half:]], lambda column: everyone), axis=0)
    corner_other = send(corner, [p for p in core_pairs if p[0] != (0, 1)])
    corner = jnp.where(core == 0, corner, corner_other)
    owner = (r == 1) & (c == 1)
    corner = jnp.where(owner, swapped, corner)

    count = 4
    quarter = tile // count
    row_first, row_second = slots[0], slots[0]
    back = send(
        slots[0], [((a, 1), (a, 0)) for a in range(rows) if a >= min(cols, rows - 1)]
    )
    row_second = jnp.where(c == 0, back, row_second)
    own_parts = [slots[0][i * quarter : (i + 1) * quarter] for i in range(count)]
    got = {}
    steps = max(cols - 2 + 2 * count - 1, count)
    for s in range(1, steps + 1):
        pairs = []
        value = own_parts[min(s - 1, count - 1)]
        for column in range(cols - 1):
            index = s - 1 if column == 0 else s - column
            limit = count if column == 0 else 2 * count
            if not 0 <= index < limit:
                continue
            for a in range(rows):
                if a >= 2 or (a == 0 and column == 0):
                    pairs.append(((a, column), (a, column + 1)))
        if s > count and cols > 2 and s - count in got:
            value = jnp.where(c == 1, got[s - count], value)
        if s > 1:
            value = jnp.where(c >= 2, got[s - 1], value)
        got[s] = send(value, pairs)
    def collected(offset_of):
        parts = []
        for i in range(count):
            part = None
            for column in range(1, cols):
                s = offset_of(column, i)
                if s is None:
                    continue
                part = got[s] if part is None else jnp.where(c == column, got[s], part)
            parts.append(part)
        return jnp.concatenate(parts, axis=0)
    firsts = collected(lambda column, i: i + 1 if column == 1 else column - 1 + count + i)
    seconds = collected(lambda column, i: None if column == 1 else column - 1 + i)
    row_first = jnp.where(c == 0, slots[0], firsts)
    row_second = jnp.where(c == 0, back, jnp.where(c == 1, slots[0], seconds))

    panel_corner_t = nn(diag_inverse, corner)
    diag_tile = jnp.where(owner, slots[0] - tn(panel_corner_t, panel_corner_t), 0.0)
    packed = factor(owner.astype(jnp.int32).reshape(1), diag_tile)
    odd = packed
    for b in range(cols):
        if b != 1:
            odd = jnp.where(c == b, send(packed, [((1, 1), (1, b))]), odd)
    for bit in bits:
        pairs = [
            ((2 * q + 1, b), (2 * (q | bit) + 1, b))
            for q in range(bit)
            for b in range(cols)
            if (q | bit) < chips
        ]
        odd = jnp.where((chip & bit) != 0, send(odd, pairs), odd)
    even = send(odd, [(y, x) for x, y in core_pairs])
    packed = jnp.where(core == 0, even, odd)
    inverse = lower_part(packed)

    panel_first = nt(row_first, diag_inverse)
    panel_first = jnp.where(r == 1, panel_corner_t.T, panel_first)
    schur = row_second - nn(panel_first, panel_corner_t)
    panel_second = nt(schur, inverse)
    row_ids = lax.broadcasted_iota(jnp.int32, packed.shape, 0)
    lane_ids = lax.broadcasted_iota(jnp.int32, packed.shape, 1)
    upper = jnp.where(lane_ids > row_ids, packed, 0.0)
    upper = upper + jnp.where(lane_ids == row_ids, 1.0 / packed, 0.0)
    panel_second = jnp.where(r == 1, upper.T, panel_second)
    panel_second = jnp.where(r >= 1, panel_second, 0.0)

    finals = [jnp.zeros_like(slots[m]) for m in range(cycles)]
    results = []
    for t in range(cycles):
        first_t = nn(diag_inverse, col_first[t])
        second_t = nn(inverse, col_second[t] - tn(panel_corner_t, first_t))
        results.append(held(t) - nn(panel_first, first_t) - nn(panel_second, second_t))
    for m in range(cycles):
        value = results[m]
        if m:
            value = jnp.where(c < 2, results[m - 1], value)
        column = m * cols + c
        finals[m] = jnp.where((r >= column) & (column >= 2), value, 0.0)
    trailing = jnp.stack(finals, axis=1)

    width = 2 * tile // cols
    both_panels = jnp.concatenate([panel_first, panel_second], axis=1)
    panels = lax.dynamic_slice_in_dim(both_panels, c * width, width, 1)
    return panels, trailing


def solution(mesh):
    rows, cols = mesh.shape["row"], mesh.shape["col"]
    return jax.shard_map(
        functools.partial(local, rows=rows, cols=cols),
        mesh=mesh,
        in_specs=(P("row", None, "col"), P()),
        out_specs=(P("row", "col"), P("row", None, "col")),
        check_vma=False,
    )
```

```python
import functools

import jax
import jax.numpy as jnp
from jax import lax
from jax.experimental import pallas as pl
from jax.experimental.pallas import tpu as pltpu
from jax.sharding import PartitionSpec as P

HIGHEST = lax.Precision.HIGHEST
AXES = ("row", "col")
SUB = 8


def dot(left, right, lhs_dim, rhs_dim):
    return lax.dot_general(
        left,
        right,
        (((lhs_dim,), (rhs_dim,)), ((), ())),
        precision=HIGHEST,
        preferred_element_type=jnp.float32,
    )


def nn(left, right):
    return dot(left, right, 1, 0)


def nt(left, right):
    return dot(left, right, 1, 1)


def tn(left, right):
    return dot(left, right, 0, 0)


def factor_block(work, aug, up):
    size = work.shape[0]
    groups = size // SUB
    rows = lax.broadcasted_iota(jnp.int32, (SUB, size), 0)
    lanes = lax.broadcasted_iota(jnp.int32, (SUB, size), 1)
    for t in range(groups):
        aug[t * SUB : (t + 1) * SUB, :] = jnp.where(lanes == rows + t * SUB, 1.0, 0.0)

    def lane(value, index):
        return jnp.broadcast_to(value[:, index : index + 1], (SUB, size))

    def row(value, index):
        return jnp.broadcast_to(value[index : index + 1, :], (SUB, size))

    for s in range(groups):
        here = slice(s * SUB, (s + 1) * SUB)
        own, own_aug = work[here, :], aug[here, :]
        columns = [lane(own, s * SUB + b) for b in range(SUB)]
        small = [[row(columns[b], a) if a >= b else None for b in range(SUB)] for a in range(SUB)]
        upper = [row(own, i) for i in range(SUB)]
        inverse = [row(own_aug, i) for i in range(SUB)]
        low = [[None] * SUB for _ in range(SUB)]
        scale = []
        for i in range(SUB):
            scale.append(lax.rsqrt(small[i][i]))
            for a in range(i + 1, SUB):
                low[a][i] = small[a][i] * scale[i]
            for b in range(i + 1, SUB):
                for a in range(b, SUB):
                    small[a][b] = small[a][b] - low[a][i] * low[b][i]
            upper[i] = upper[i] * scale[i]
            inverse[i] = inverse[i] * scale[i]
            for b in range(i + 1, SUB):
                upper[b] = upper[b] - upper[i] * low[b][i]
                inverse[b] = inverse[b] - inverse[i] * low[b][i]
        for t in range(s + 1, groups):
            there = slice(t * SUB, (t + 1) * SUB)
            current, current_aug = work[there, :], aug[there, :]
            part = [lane(current, s * SUB + b) for b in range(SUB)]
            for i in range(SUB):
                part[i] = part[i] * scale[i]
                for b in range(i + 1, SUB):
                    part[b] = part[b] - part[i] * low[b][i]
                current = current - part[i] * upper[i]
                current_aug = current_aug - part[i] * inverse[i]
            work[there, :] = current
            aug[there, :] = current_aug
        packed_inverse, packed_upper = inverse[0], upper[0]
        for i in range(1, SUB):
            packed_inverse = jnp.where(rows == i, inverse[i], packed_inverse)
            packed_upper = jnp.where(rows == i, upper[i], packed_upper)
        aug[here, :] = packed_inverse
        up[here, :] = jnp.where(lanes >= rows + s * SUB, packed_upper, 0.0)


def factor_pair(work, diag, aug, up, inv_ref, up_ref):
    size = work.shape[0]
    part = size // 2
    low, high = slice(0, part), slice(part, size)
    diag[...] = work[low, low]

    def step(k, carry):
        factor_block(diag, aug, up)

        @pl.when(k == 0)
        def _():
            inv = aug[...]
            cross = nn(inv, work[low, high])
            diag[...] = work[high, high] - tn(cross, cross)
            inv_ref[low, low] = inv
            inv_ref[low, high] = jnp.zeros_like(inv)
            up_ref[low, low] = up[...]
            up_ref[low, high] = cross

        @pl.when(k == 1)
        def _():
            inv = aug[...]
            inv_ref[high, high] = inv
            inv_ref[high, low] = -nn(inv, tn(up_ref[low, high], inv_ref[low, low]))
            up_ref[high, high] = up[...]
            up_ref[high, low] = jnp.zeros_like(inv)

        return carry

    lax.fori_loop(0, 2, step, 0)


def packed_of(inverse, upper):
    rows = lax.broadcasted_iota(jnp.int32, inverse.shape, 0)
    lanes = lax.broadcasted_iota(jnp.int32, inverse.shape, 1)
    return jnp.where(lanes <= rows, inverse, upper)


def lower_part(packed):
    rows = lax.broadcasted_iota(jnp.int32, packed.shape, 0)
    lanes = lax.broadcasted_iota(jnp.int32, packed.shape, 1)
    return jnp.where(lanes <= rows, packed, 0.0)


def factor_of(packed):
    rows = lax.broadcasted_iota(jnp.int32, packed.shape, 0)
    lanes = lax.broadcasted_iota(jnp.int32, packed.shape, 1)
    inverse_diag = jnp.where(lanes == rows, 1.0 / packed, 0.0)
    return jnp.where(lanes > rows, packed, inverse_diag).T


def place():
    return lax.axis_index("row"), lax.axis_index("col")


def fetch(target, semaphore, choices):
    for condition, source in choices:

        @pl.when(condition)
        def _(source=source):
            pltpu.make_async_copy(source, target, semaphore).start()

    return pltpu.make_async_copy(choices[0][1], target, semaphore).wait


def call(kernel, name, out_shapes, inputs, scratch, in_vmem=False, flops=0):
    outs = [jax.ShapeDtypeStruct(shape, jnp.float32) for shape in out_shapes]
    size = sum(4 * x.size for x in inputs) + sum(4 * x.size for x in outs)
    return pl.pallas_call(
        kernel,
        out_shape=outs,
        in_specs=[pl.BlockSpec(memory_space=pltpu.VMEM if in_vmem else pl.ANY)] * len(inputs),
        out_specs=[pl.BlockSpec(memory_space=pltpu.VMEM)] * len(outs),
        scratch_shapes=scratch,
        cost_estimate=pl.CostEstimate(flops=flops, bytes_accessed=size, transcendentals=0),
        name=name,
    )(*inputs)


def vmem(*shape):
    return pltpu.VMEM(shape, jnp.float32)


def copies(count):
    return pltpu.SemaphoreType.DMA((count,))


def split(refs, *counts):
    groups = []
    for count in counts:
        groups.append(refs[:count])
        refs = refs[count:]
    return groups


def extract_kernel(cov_ref, own_ref, low_ref, high_ref, *held_refs):
    half = low_ref.shape[0]
    cycles = cov_ref.shape[1]
    _, c = place()
    own = cov_ref[:, 0, :]
    own_ref[...] = own
    low_ref[...] = own[:half]
    high_ref[...] = own[half:]
    for t, held_ref in enumerate(held_refs):
        later = cov_ref[:, min(t + 1, cycles - 1), :]
        held_ref[...] = jnp.where(c < 2, later, cov_ref[:, t, :])


def factor_scratch(half):
    part = half // 2
    shapes = [(half, half), (part, part), (part, part), (part, part), (half, half), (half, half)]
    return [vmem(*shape) for shape in shapes]


def first_kernel(
    swapped_ref, own_ref, diag_ref, out_ref, rest_ref,
    corner, second, dinv, work, diag, aug, up, inv, upper, sems,
):
    half = out_ref.shape[0]
    r, c = place()
    owner = (r == 1) & (c == 1)

    @pl.when(owner)
    def _():
        waits = [
            fetch(corner, sems.at[0], [(owner, swapped_ref)]),
            fetch(dinv, sems.at[1], [(owner, diag_ref)]),
            fetch(second, sems.at[2], [(owner, own_ref)]),
        ]
        for wait in waits:
            wait()
        panel = nn(dinv[...], corner[...])
        second[...] = second[...] - tn(panel, panel)
        work[...] = second[:half, :half]
        factor_pair(work, diag, aug, up, inv, upper)
        cross = nn(inv[...], second[:half, half:])
        rest_ref[...] = second[half:, half:] - tn(cross, cross)
        out_ref[:, :half] = packed_of(inv[...], upper[...])
        out_ref[:, half:] = cross


def second_kernel(rest_ref, out_ref, work, diag, aug, up, inv, upper, sems):
    r, c = place()
    owner = (r == 1) & (c == 1)

    @pl.when(owner)
    def _():
        fetch(work, sems.at[0], [(owner, rest_ref)])()
        factor_pair(work, diag, aug, up, inv, upper)
        out_ref[...] = packed_of(inv[...], upper[...])


def early_kernel(cols, tiles, *refs):
    hops = cols - 1
    (own, back, diag), low, high, mine, other, held, (panel_ref, second_ref), first_t, part, rest = split(
        refs, 3, hops, hops, tiles, tiles, tiles, 2, tiles, tiles, 4
    )
    first, dinv, column, sems = rest
    half = low[0].shape[0]
    r, c = place()
    core = r % 2
    always = c >= 0
    waits = [fetch(dinv, sems.at[0], [(always, diag)])]
    for i, parts in enumerate((low, high)):
        rows = pl.ds(i * half, half)
        choices = [(c == 0, own.at[rows])]
        choices += [(c == b, parts[b - 1]) for b in range(1, cols)]
        waits.append(fetch(first.at[rows], sems.at[1 + i], choices))
        choices = [(c == 0, back.at[rows]), (c == 1, own.at[rows])]
        choices += [(c == b, parts[b - 2]) for b in range(2, cols)]
        waits.append(fetch(second_ref.at[rows], sems.at[3 + i], choices))
    for wait in waits:
        wait()
    panel_ref[...] = nt(first[...], dinv[...])
    for t in range(tiles):
        index = (t + jnp.where(c < 2, 1, 0)) * cols + c

        @pl.when(r >= index)
        def _(t=t):
            waits = [
                fetch(column, sems.at[5], [(core == 0, mine[t]), (core == 1, other[t])]),
                fetch(part[t], sems.at[6], [(always, held[t])]),
            ]
            for wait in waits:
                wait()
            first_t[t][...] = nn(dinv[...], column[...])
            part[t][...] = part[t][...] - nn(panel_ref[...], first_t[t][...])


def middle_kernel(cols, tiles, *refs):
    (even, odd, diag, panel, second), mine, other, first_t, (panel_ref, schur_ref), schur_t, rest = split(
        refs, 5, tiles, tiles, tiles, 2, tiles, 5
    )
    corner, dinv, corner_panel, column, sems = rest
    r, c = place()
    core = r % 2
    always = c >= 0
    waits = [
        fetch(dinv, sems.at[0], [(always, diag)]),
        fetch(corner, sems.at[1], [(core == 0, even), (core == 1, odd)]),
        fetch(panel_ref, sems.at[2], [(always, panel)]),
        fetch(schur_ref, sems.at[3], [(always, second)]),
    ]
    for wait in waits:
        wait()
    corner_panel[...] = nn(dinv[...], corner[...])

    @pl.when(r == 1)
    def _():
        panel_ref[...] = corner_panel[...].T

    schur_ref[...] = schur_ref[...] - nn(panel_ref[...], corner_panel[...])
    for t in range(tiles):
        index = (t + jnp.where(c < 2, 1, 0)) * cols + c

        @pl.when(r >= index)
        def _(t=t):
            waits = [
                fetch(column, sems.at[4], [(always, first_t[t])]),
                fetch(schur_t[t], sems.at[5], [(core == 1, mine[t]), (core == 0, other[t])]),
            ]
            for wait in waits:
                wait()
            schur_t[t][...] = schur_t[t][...] - tn(corner_panel[...], column[...])


def late_kernel(cols, cycles, tiles, *refs):
    (even0, odd0, even1, odd1, panel, schur, near_panel, near_schur, held), first_part, schur_t, outs, rest = split(
        refs, 9, tiles, tiles, 2, 9
    )
    panels_ref, trailing_ref = outs
    piece, corner, first, second, other, other_second, column, total, sems = rest
    half = corner.shape[0]
    low, high = slice(0, half), slice(half, 2 * half)
    r, c = place()
    core = r % 2
    always = c >= 0
    last = (cycles - 1) * cols + c
    near = (c >= 2) & (r // 2 == last // 2) & (r >= last)
    waits = [
        fetch(piece, sems.at[0], [(core == 0, even0), (core == 1, odd0)]),
        fetch(corner, sems.at[1], [(core == 0, even1), (core == 1, odd1)]),
        fetch(first, sems.at[2], [(always, panel)]),
        fetch(second, sems.at[3], [(always, schur)]),
    ]
    for wait in waits:
        wait()

    def solve(target):
        target[:, low] = nt(target[:, low], lower_part(piece[:, low]))
        update = target[:, high] - nn(target[:, low], piece[:, high])
        target[:, high] = nt(update, lower_part(corner[...]))

    solve(second)

    @pl.when(r == 0)
    def _():
        second[...] = jnp.zeros_like(second)

    @pl.when(r == 1)
    def _():
        second[low, low] = factor_of(piece[:, low])
        second[low, high] = jnp.zeros((half, half), jnp.float32)
        second[high, low] = piece[:, high].T
        second[high, high] = factor_of(corner[...])

    width = panels_ref.shape[1]
    for b in range(cols):

        @pl.when(c == b)
        def _(b=b):
            source, start = (first, b * width) if 2 * b < cols else (second, b * width - 2 * half)
            panels_ref[...] = source[:, start : start + width]

    trailing_ref[...] = jnp.zeros_like(trailing_ref)

    def store(t):
        for shift in (0, 1):
            if t + shift < cycles:

                @pl.when((c < 2) if shift else (c >= 2))
                def _(slot=t + shift):
                    trailing_ref[:, slot, :] = total[...]

    for t in range(tiles):
        index = (t + jnp.where(c < 2, 1, 0)) * cols + c
        wanted = r >= index
        if t + 1 == cycles:
            wanted = wanted & jnp.logical_not(near)

        @pl.when(wanted)
        def _(t=t):
            waits = [
                fetch(column, sems.at[4], [(always, schur_t[t])]),
                fetch(total, sems.at[5], [(always, first_part[t])]),
            ]
            for wait in waits:
                wait()
            column[low] = nn(lower_part(piece[:, low]), column[low])
            update = column[high] - tn(piece[:, high], column[low])
            column[high] = nn(lower_part(corner[...]), update)
            total[...] = total[...] - nn(second[...], column[...])
            store(t)

    @pl.when(near)
    def _():
        own = r == last
        waits = [
            fetch(other, sems.at[6], [(own, panel), (r != last, near_panel)]),
            fetch(other_second, sems.at[7], [(own, schur), (r != last, near_schur)]),
            fetch(total, sems.at[5], [(always, held)]),
        ]
        for wait in waits:
            wait()
        solve(other_second)
        value = total[...] - nt(first[...], other[...])
        total[...] = value - nt(second[...], other_second[...])
        store(cycles - 1)


def local(covariance, diag_inverse, rows, cols):
    tile = covariance.shape[0]
    cycles = covariance.shape[1]
    half = tile // 2
    chips = rows // 2
    r, c = place()
    chip, core = r // 2, r % 2
    whole = (tile, tile)

    def send(value, pairs):
        flat = [(a * cols + b, x * cols + y) for (a, b), (x, y) in pairs]
        return lax.ppermute(value, AXES, flat)

    bits = []
    while (1 << len(bits)) < chips:
        bits.append(1 << len(bits))

    def column_of(t, column):
        return (t + (1 if column < 2 else 0)) * cols + column

    own, own_low, own_high, *held = call(
        extract_kernel,
        "extract",
        [whole, (half, tile), (half, tile)] + [whole] * cycles,
        [covariance],
        [],
        in_vmem=True,
    )

    with jax.named_scope("swap"):
        swapped = send(own, [((0, 1), (1, 1))])

    def along(column, hop):
        pairs = []
        source = column - hop
        for a in range(rows):
            lead = a >= 2 and source in (0, 1)
            if lead or (a == 0 and (source == 1 or (source == 0 and hop == 0))):
                pairs.append(((a, column), (a, column + 1)))
        return pairs

    moved = []
    for name, part in (("low", own_low), ("high", own_high)):
        chain = []
        for hop in range(cols - 1):
            pairs = [pair for column in range(cols - 1) for pair in along(column, hop)]
            with jax.named_scope(f"along_{name}_{hop}"):
                part = send(part, pairs)
            chain.append(part)
        moved.append(chain)
    with jax.named_scope("back"):
        back = send(
            own, [((a, 1), (a, 0)) for a in range(rows) if a == 0 or a >= min(cols, rows - 1)]
        )

    def spread(value, wanted, cores, name):
        current = value
        for step in range(len(bits)):
            pairs = []
            arrived = False
            for k in cores:
                order = bits if k == 0 else bits[::-1]
                used, bit, later = sum(order[:step]), order[step], sum(order[step + 1 :])
                arrived = jnp.where(core == k, (chip & bit) != 0, arrived)
                for column in range(cols):
                    for q in range(chips):
                        target = q | bit
                        if q & ~used or target >= chips:
                            continue
                        reach = {target | extra for extra in range(chips) if not extra & ~later}
                        if reach & wanted(column):
                            pairs.append(((2 * q + k, column), (2 * target + k, column)))
            if pairs:
                with jax.named_scope(f"{name}_{step}"):
                    current = jnp.where(arrived, send(current, pairs), current)
        return current

    def trade(value, wanted, name, ways=(0, 1)):
        pairs = []
        for column in range(cols):
            for q in wanted(column):
                pairs += [((2 * q + k, column), (2 * q + 1 - k, column)) for k in ways]
        with jax.named_scope(name):
            return send(value, pairs)

    mine, other = [], []
    for t in range(cycles):

        def wanted(column, t=t):
            if column < 2 and t + 1 >= cycles:
                return set()
            edge = column_of(t, column) // 2 + (1 if t + 1 == cycles else 0)
            return {q for q in range(chips) if q >= edge and q > 0}

        if any(wanted(column) for column in range(cols)):
            mine.append(spread(held[t], wanted, (0, 1), f"column_{t}"))
            other.append(trade(mine[-1], wanted, f"column_trade_{t}"))
    tiles = len(mine)

    first_piece, remainder = call(
        first_kernel,
        "factor_first",
        [(half, tile), (half, half)],
        [swapped, own, diag_inverse],
        [vmem(*whole)] * 3 + factor_scratch(half) + [copies(3)],
    )
    second_piece = call(
        second_kernel,
        "factor_second",
        [(half, half)],
        [remainder],
        factor_scratch(half) + [copies(1)],
    )[0]

    def everyone(column):
        return set(range(chips))

    corner = jnp.where(c == 0, back, own)
    for b in range(2, cols):
        arrived = jnp.concatenate([moved[0][b - 2], moved[1][b - 2]], axis=0)
        corner = jnp.where(c == b, arrived, corner)
    corner = spread(corner, everyone, (0,), "corner")
    corner_odd = trade(corner, everyone, "corner_trade", (0,))

    def distribute(piece, name):
        current = piece
        for b in range(cols):
            if b != 1:
                with jax.named_scope(f"{name}_to_{b}"):
                    current = jnp.where(c == b, send(piece, [((1, 1), (1, b))]), current)
        current = spread(current, everyone, (1,), name)
        return current, trade(current, everyone, f"{name}_trade", (1,))

    first_odd, first_even = distribute(first_piece, "first_piece")
    second_odd, second_even = distribute(second_piece, "second_piece")

    product = 2 * tile**3
    panel, second, *products = call(
        functools.partial(early_kernel, cols, tiles),
        "early",
        [whole] * (2 + 2 * tiles),
        [own, back, diag_inverse, *moved[0], *moved[1], *mine, *other, *held[:tiles]],
        [vmem(*whole)] * 3 + [copies(7)],
        flops=3 * product,
    )
    first_t, partial = products[:tiles], products[tiles:]
    panel, schur, *schur_t = call(
        functools.partial(middle_kernel, cols, tiles),
        "middle",
        [whole] * (2 + tiles),
        [corner, corner_odd, diag_inverse, panel, second, *mine, *other, *first_t],
        [vmem(*whole)] * 4 + [copies(6)],
        flops=3 * product,
    )
    edges = [column_of(cycles - 1, b) for b in range(2, cols)]
    pairs = [((j, b), (j + 1, b)) for b, j in zip(range(2, cols), edges) if j % 2 == 0]
    with jax.named_scope("near_panel"):
        near_panel = send(panel, pairs)
    with jax.named_scope("near_schur"):
        near_schur = send(schur, pairs)
    panels, trailing = call(
        functools.partial(late_kernel, cols, cycles, tiles),
        "late",
        [(tile, 2 * tile // cols), covariance.shape],
        [
            first_even, first_odd, second_even, second_odd,
            panel, schur, near_panel, near_schur, held[-1], *partial, *schur_t,
        ],
        [vmem(half, tile), vmem(half, half)] + [vmem(*whole)] * 6 + [copies(8)],
        flops=4 * product,
    )
    return panels, trailing


def solution(mesh):
    rows, cols = mesh.shape["row"], mesh.shape["col"]
    return jax.shard_map(
        functools.partial(local, rows=rows, cols=cols),
        mesh=mesh,
        in_specs=(P("row", None, "col"), P()),
        out_specs=(P("row", "col"), P("row", None, "col")),
        check_vma=False,
    )
```

```python
import functools

import jax
import jax.numpy as jnp
from jax import lax
from jax.experimental import pallas as pl
from jax.experimental.pallas import tpu as pltpu
from jax.sharding import PartitionSpec as P

HIGHEST = lax.Precision.HIGHEST
AXES = ("row", "col")
SUB = 8


def dot(left, right, lhs_dim, rhs_dim):
    return lax.dot_general(
        left,
        right,
        (((lhs_dim,), (rhs_dim,)), ((), ())),
        precision=HIGHEST,
        preferred_element_type=jnp.float32,
    )


def nn(left, right):
    return dot(left, right, 1, 0)


def nt(left, right):
    return dot(left, right, 1, 1)


def tn(left, right):
    return dot(left, right, 0, 0)


def factor_block(work, aug, up):
    size = work.shape[0]
    groups = size // SUB
    rows = lax.broadcasted_iota(jnp.int32, (SUB, size), 0)
    lanes = lax.broadcasted_iota(jnp.int32, (SUB, size), 1)
    for t in range(groups):
        aug[t * SUB : (t + 1) * SUB, :] = jnp.where(lanes == rows + t * SUB, 1.0, 0.0)

    def lane(value, index):
        return jnp.broadcast_to(value[:, index : index + 1], (SUB, size))

    def row(value, index):
        return jnp.broadcast_to(value[index : index + 1, :], (SUB, size))

    for s in range(groups):
        here = slice(s * SUB, (s + 1) * SUB)
        own, own_aug = work[here, :], aug[here, :]
        columns = [lane(own, s * SUB + b) for b in range(SUB)]
        small = [[row(columns[b], a) if a >= b else None for b in range(SUB)] for a in range(SUB)]
        upper = [row(own, i) for i in range(SUB)]
        inverse = [row(own_aug, i) for i in range(SUB)]
        low = [[None] * SUB for _ in range(SUB)]
        scale = []
        for i in range(SUB):
            scale.append(lax.rsqrt(small[i][i]))
            for a in range(i + 1, SUB):
                low[a][i] = small[a][i] * scale[i]
            for b in range(i + 1, SUB):
                for a in range(b, SUB):
                    small[a][b] = small[a][b] - low[a][i] * low[b][i]
            upper[i] = upper[i] * scale[i]
            inverse[i] = inverse[i] * scale[i]
            for b in range(i + 1, SUB):
                upper[b] = upper[b] - upper[i] * low[b][i]
                inverse[b] = inverse[b] - inverse[i] * low[b][i]
        for t in range(s + 1, groups):
            there = slice(t * SUB, (t + 1) * SUB)
            current, current_aug = work[there, :], aug[there, :]
            part = [lane(current, s * SUB + b) for b in range(SUB)]
            for i in range(SUB):
                part[i] = part[i] * scale[i]
                for b in range(i + 1, SUB):
                    part[b] = part[b] - part[i] * low[b][i]
                current = current - part[i] * upper[i]
                current_aug = current_aug - part[i] * inverse[i]
            work[there, :] = current
            aug[there, :] = current_aug
        packed_inverse, packed_upper = inverse[0], upper[0]
        for i in range(1, SUB):
            packed_inverse = jnp.where(rows == i, inverse[i], packed_inverse)
            packed_upper = jnp.where(rows == i, upper[i], packed_upper)
        aug[here, :] = packed_inverse
        up[here, :] = jnp.where(lanes >= rows + s * SUB, packed_upper, 0.0)


def factor_pair(work, diag, aug, up, inv_ref, up_ref):
    size = work.shape[0]
    part = size // 2
    low, high = slice(0, part), slice(part, size)
    diag[...] = work[low, low]

    def step(k, carry):
        factor_block(diag, aug, up)

        @pl.when(k == 0)
        def _():
            inv = aug[...]
            cross = nn(inv, work[low, high])
            diag[...] = work[high, high] - tn(cross, cross)
            inv_ref[low, low] = inv
            inv_ref[low, high] = jnp.zeros_like(inv)
            up_ref[low, low] = up[...]
            up_ref[low, high] = cross

        @pl.when(k == 1)
        def _():
            inv = aug[...]
            inv_ref[high, high] = inv
            inv_ref[high, low] = -nn(inv, tn(up_ref[low, high], inv_ref[low, low]))
            up_ref[high, high] = up[...]
            up_ref[high, low] = jnp.zeros_like(inv)

        return carry

    lax.fori_loop(0, 2, step, 0)


def packed_of(inverse, upper):
    rows = lax.broadcasted_iota(jnp.int32, inverse.shape, 0)
    lanes = lax.broadcasted_iota(jnp.int32, inverse.shape, 1)
    return jnp.where(lanes <= rows, inverse, upper)


def lower_part(packed):
    rows = lax.broadcasted_iota(jnp.int32, packed.shape, 0)
    lanes = lax.broadcasted_iota(jnp.int32, packed.shape, 1)
    return jnp.where(lanes <= rows, packed, 0.0)


def factor_of(packed):
    rows = lax.broadcasted_iota(jnp.int32, packed.shape, 0)
    lanes = lax.broadcasted_iota(jnp.int32, packed.shape, 1)
    inverse_diag = jnp.where(lanes == rows, 1.0 / packed, 0.0)
    return jnp.where(lanes > rows, packed, inverse_diag).T


def place():
    return lax.axis_index("row"), lax.axis_index("col")


def fetch(target, semaphore, choices):
    for condition, source in choices:

        @pl.when(condition)
        def _(source=source):
            pltpu.make_async_copy(source, target, semaphore).start()

    return pltpu.make_async_copy(choices[0][1], target, semaphore).wait


def call(kernel, out_shapes, inputs, scratch, in_vmem=False, flops=0):
    outs = [jax.ShapeDtypeStruct(shape, jnp.float32) for shape in out_shapes]
    size = sum(4 * x.size for x in inputs) + sum(4 * x.size for x in outs)
    return pl.pallas_call(
        kernel,
        out_shape=outs,
        in_specs=[pl.BlockSpec(memory_space=pltpu.VMEM if in_vmem else pl.ANY)] * len(inputs),
        out_specs=[pl.BlockSpec(memory_space=pltpu.VMEM)] * len(outs),
        scratch_shapes=scratch,
        cost_estimate=pl.CostEstimate(flops=flops, bytes_accessed=size, transcendentals=0),
    )(*inputs)


def vmem(*shape):
    return pltpu.VMEM(shape, jnp.float32)


def copies(count):
    return pltpu.SemaphoreType.DMA((count,))


def split(refs, *counts):
    groups = []
    for count in counts:
        groups.append(refs[:count])
        refs = refs[count:]
    return groups


def extract_kernel(cov_ref, own_ref, low_ref, high_ref, *held_refs):
    half = low_ref.shape[0]
    cycles = cov_ref.shape[1]
    _, c = place()
    own = cov_ref[:, 0, :]
    own_ref[...] = own
    low_ref[...] = own[:half]
    high_ref[...] = own[half:]
    for t, held_ref in enumerate(held_refs):
        later = cov_ref[:, min(t + 1, cycles - 1), :]
        held_ref[...] = jnp.where(c < 2, later, cov_ref[:, t, :])


def factor_scratch(half):
    part = half // 2
    shapes = [(half, half), (part, part), (part, part), (part, part), (half, half), (half, half)]
    return [vmem(*shape) for shape in shapes]


def first_kernel(
    swapped_ref, own_ref, diag_ref, out_ref, rest_ref,
    corner, second, dinv, work, diag, aug, up, inv, upper, sems,
):
    half = out_ref.shape[0]
    r, c = place()
    owner = (r == 1) & (c == 1)

    @pl.when(owner)
    def _():
        waits = [
            fetch(corner, sems.at[0], [(owner, swapped_ref)]),
            fetch(dinv, sems.at[1], [(owner, diag_ref)]),
            fetch(second, sems.at[2], [(owner, own_ref)]),
        ]
        for wait in waits:
            wait()
        panel = nn(dinv[...], corner[...])
        second[...] = second[...] - tn(panel, panel)
        work[...] = second[:half, :half]
        factor_pair(work, diag, aug, up, inv, upper)
        cross = nn(inv[...], second[:half, half:])
        rest_ref[...] = second[half:, half:] - tn(cross, cross)
        out_ref[:, :half] = packed_of(inv[...], upper[...])
        out_ref[:, half:] = cross


def second_kernel(rest_ref, out_ref, work, diag, aug, up, inv, upper, sems):
    r, c = place()
    owner = (r == 1) & (c == 1)

    @pl.when(owner)
    def _():
        fetch(work, sems.at[0], [(owner, rest_ref)])()
        factor_pair(work, diag, aug, up, inv, upper)
        out_ref[...] = packed_of(inv[...], upper[...])


def early_kernel(cols, tiles, *refs):
    hops = cols - 1
    (own, back, diag), low, high, mine, other, held, (panel_ref, second_ref), first_t, part, rest = split(
        refs, 3, hops, hops, tiles, tiles, tiles, 2, tiles, tiles, 4
    )
    first, dinv, column, sems = rest
    half = low[0].shape[0]
    r, c = place()
    core = r % 2
    always = c >= 0
    waits = [fetch(dinv, sems.at[0], [(always, diag)])]
    for i, parts in enumerate((low, high)):
        rows = pl.ds(i * half, half)
        choices = [(c == 0, own.at[rows])]
        choices += [(c == b, parts[b - 1]) for b in range(1, cols)]
        waits.append(fetch(first.at[rows], sems.at[1 + i], choices))
        choices = [(c == 0, back.at[rows]), (c == 1, own.at[rows])]
        choices += [(c == b, parts[b - 2]) for b in range(2, cols)]
        waits.append(fetch(second_ref.at[rows], sems.at[3 + i], choices))
    for wait in waits:
        wait()
    panel_ref[...] = nt(first[...], dinv[...])
    for t in range(tiles):
        index = (t + jnp.where(c < 2, 1, 0)) * cols + c

        @pl.when(r >= index)
        def _(t=t):
            waits = [
                fetch(column, sems.at[5], [(core == 0, mine[t]), (core == 1, other[t])]),
                fetch(part[t], sems.at[6], [(always, held[t])]),
            ]
            for wait in waits:
                wait()
            first_t[t][...] = nn(dinv[...], column[...])
            part[t][...] = part[t][...] - nn(panel_ref[...], first_t[t][...])


def middle_kernel(cols, tiles, *refs):
    (even, odd, diag, panel, second), mine, other, first_t, (panel_ref, schur_ref), schur_t, rest = split(
        refs, 5, tiles, tiles, tiles, 2, tiles, 5
    )
    corner, dinv, corner_panel, column, sems = rest
    r, c = place()
    core = r % 2
    always = c >= 0
    waits = [
        fetch(dinv, sems.at[0], [(always, diag)]),
        fetch(corner, sems.at[1], [(core == 0, even), (core == 1, odd)]),
        fetch(panel_ref, sems.at[2], [(always, panel)]),
        fetch(schur_ref, sems.at[3], [(always, second)]),
    ]
    for wait in waits:
        wait()
    corner_panel[...] = nn(dinv[...], corner[...])

    @pl.when(r == 1)
    def _():
        panel_ref[...] = corner_panel[...].T

    schur_ref[...] = schur_ref[...] - nn(panel_ref[...], corner_panel[...])
    for t in range(tiles):
        index = (t + jnp.where(c < 2, 1, 0)) * cols + c

        @pl.when(r >= index)
        def _(t=t):
            waits = [
                fetch(column, sems.at[4], [(always, first_t[t])]),
                fetch(schur_t[t], sems.at[5], [(core == 1, mine[t]), (core == 0, other[t])]),
            ]
            for wait in waits:
                wait()
            schur_t[t][...] = schur_t[t][...] - tn(corner_panel[...], column[...])


def late_kernel(cols, cycles, tiles, *refs):
    (even0, odd0, even1, odd1, panel, schur, near_panel, near_schur, held), first_part, schur_t, outs, rest = split(
        refs, 9, tiles, tiles, 2, 9
    )
    panels_ref, trailing_ref = outs
    piece, corner, first, second, other, other_second, column, total, sems = rest
    half = corner.shape[0]
    low, high = slice(0, half), slice(half, 2 * half)
    r, c = place()
    core = r % 2
    always = c >= 0
    last = (cycles - 1) * cols + c
    near = (c >= 2) & (r // 2 == last // 2) & (r >= last)
    waits = [
        fetch(piece, sems.at[0], [(core == 0, even0), (core == 1, odd0)]),
        fetch(corner, sems.at[1], [(core == 0, even1), (core == 1, odd1)]),
        fetch(first, sems.at[2], [(always, panel)]),
        fetch(second, sems.at[3], [(always, schur)]),
    ]
    for wait in waits:
        wait()

    def solve(target):
        target[:, low] = nt(target[:, low], lower_part(piece[:, low]))
        update = target[:, high] - nn(target[:, low], piece[:, high])
        target[:, high] = nt(update, lower_part(corner[...]))

    solve(second)

    @pl.when(r == 0)
    def _():
        second[...] = jnp.zeros_like(second)

    @pl.when(r == 1)
    def _():
        second[low, low] = factor_of(piece[:, low])
        second[low, high] = jnp.zeros((half, half), jnp.float32)
        second[high, low] = piece[:, high].T
        second[high, high] = factor_of(corner[...])

    width = panels_ref.shape[1]
    for b in range(cols):

        @pl.when(c == b)
        def _(b=b):
            source, start = (first, b * width) if 2 * b < cols else (second, b * width - 2 * half)
            panels_ref[...] = source[:, start : start + width]

    trailing_ref[...] = jnp.zeros_like(trailing_ref)

    def store(t):
        for shift in (0, 1):
            if t + shift < cycles:

                @pl.when((c < 2) if shift else (c >= 2))
                def _(slot=t + shift):
                    trailing_ref[:, slot, :] = total[...]

    for t in range(tiles):
        index = (t + jnp.where(c < 2, 1, 0)) * cols + c
        wanted = r >= index
        if t + 1 == cycles:
            wanted = wanted & jnp.logical_not(near)

        @pl.when(wanted)
        def _(t=t):
            waits = [
                fetch(column, sems.at[4], [(always, schur_t[t])]),
                fetch(total, sems.at[5], [(always, first_part[t])]),
            ]
            for wait in waits:
                wait()
            column[low] = nn(lower_part(piece[:, low]), column[low])
            update = column[high] - tn(piece[:, high], column[low])
            column[high] = nn(lower_part(corner[...]), update)
            total[...] = total[...] - nn(second[...], column[...])
            store(t)

    @pl.when(near)
    def _():
        own = r == last
        waits = [
            fetch(other, sems.at[6], [(own, panel), (r != last, near_panel)]),
            fetch(other_second, sems.at[7], [(own, schur), (r != last, near_schur)]),
            fetch(total, sems.at[5], [(always, held)]),
        ]
        for wait in waits:
            wait()
        solve(other_second)
        value = total[...] - nt(first[...], other[...])
        total[...] = value - nt(second[...], other_second[...])
        store(cycles - 1)


def local(covariance, diag_inverse, rows, cols):
    tile = covariance.shape[0]
    cycles = covariance.shape[1]
    half = tile // 2
    chips = rows // 2
    r, c = place()
    chip, core = r // 2, r % 2
    whole = (tile, tile)

    def send(value, pairs):
        flat = [(a * cols + b, x * cols + y) for (a, b), (x, y) in pairs]
        return lax.ppermute(value, AXES, flat)

    bits = []
    while (1 << len(bits)) < chips:
        bits.append(1 << len(bits))

    def column_of(t, column):
        return (t + (1 if column < 2 else 0)) * cols + column

    own, own_low, own_high, *held = call(
        extract_kernel,
        [whole, (half, tile), (half, tile)] + [whole] * cycles,
        [covariance],
        [],
        in_vmem=True,
    )

    swapped = send(own, [((0, 1), (1, 1))])

    def along(column, hop):
        source = column - hop
        return [
            ((a, column), (a, column + 1))
            for a in range(rows)
            if (a >= 2 and source in (0, 1)) or (a == 0 and source == 0 and hop == 0)
        ]

    moved = []
    for part in (own_low, own_high):
        chain = []
        for hop in range(cols - 1):
            pairs = [pair for column in range(cols - 1) for pair in along(column, hop)]
            part = send(part, pairs)
            chain.append(part)
        moved.append(chain)
    back = send(
        own, [((a, 1), (a, 0)) for a in range(rows) if a >= min(cols, rows - 1)]
    )

    def spread(value, wanted, cores):
        current = value
        for step in range(len(bits)):
            pairs = []
            arrived = False
            for k in cores:
                order = bits if k == 0 else bits[::-1]
                used, bit, later = sum(order[:step]), order[step], sum(order[step + 1 :])
                arrived = jnp.where(core == k, (chip & bit) != 0, arrived)
                for column in range(cols):
                    for q in range(chips):
                        target = q | bit
                        if q & ~used or target >= chips:
                            continue
                        reach = {target | extra for extra in range(chips) if not extra & ~later}
                        if reach & wanted(column):
                            pairs.append(((2 * q + k, column), (2 * target + k, column)))
            if pairs:
                current = jnp.where(arrived, send(current, pairs), current)
        return current

    def trade(value, wanted, ways=(0, 1)):
        pairs = []
        for column in range(cols):
            for q in wanted(column):
                pairs += [((2 * q + k, column), (2 * q + 1 - k, column)) for k in ways]
        return send(value, pairs)

    mine, other = [], []
    for t in range(cycles):

        def wanted(column, t=t):
            if column < 2 and t + 1 >= cycles:
                return set()
            edge = column_of(t, column) // 2 + (1 if t + 1 == cycles else 0)
            return {q for q in range(chips) if q >= edge and q > 0}

        if any(wanted(column) for column in range(cols)):
            mine.append(spread(held[t], wanted, (0, 1)))
            other.append(trade(mine[-1], wanted))
    tiles = len(mine)

    first_piece, remainder = call(
        first_kernel,
        [(half, tile), (half, half)],
        [swapped, own, diag_inverse],
        [vmem(*whole)] * 3 + factor_scratch(half) + [copies(3)],
    )
    second_piece = call(
        second_kernel, [(half, half)], [remainder], factor_scratch(half) + [copies(1)]
    )[0]

    def everyone(column):
        return set(range(chips))

    corner = own
    for b in range(cols):
        if b != 1:
            corner = jnp.where(c == b, send(own, [((0, 1), (0, b))]), corner)
    corner = spread(corner, everyone, (0,))
    corner_odd = trade(corner, everyone, (0,))

    def distribute(piece):
        current = piece
        for b in range(cols):
            if b != 1:
                current = jnp.where(c == b, send(piece, [((1, 1), (1, b))]), current)
        current = spread(current, everyone, (1,))
        return current, trade(current, everyone, (1,))

    first_odd, first_even = distribute(first_piece)
    second_odd, second_even = distribute(second_piece)

    product = 2 * tile**3
    panel, second, *products = call(
        functools.partial(early_kernel, cols, tiles),
        [whole] * (2 + 2 * tiles),
        [own, back, diag_inverse, *moved[0], *moved[1], *mine, *other, *held[:tiles]],
        [vmem(*whole)] * 3 + [copies(7)],
        flops=3 * product,
    )
    first_t, partial = products[:tiles], products[tiles:]
    panel, schur, *schur_t = call(
        functools.partial(middle_kernel, cols, tiles),
        [whole] * (2 + tiles),
        [corner, corner_odd, diag_inverse, panel, second, *mine, *other, *first_t],
        [vmem(*whole)] * 4 + [copies(6)],
        flops=3 * product,
    )
    edges = [column_of(cycles - 1, b) for b in range(2, cols)]
    pairs = [((j, b), (j + 1, b)) for b, j in zip(range(2, cols), edges) if j % 2 == 0]
    near_panel = send(panel, pairs)
    near_schur = send(schur, pairs)
    panels, trailing = call(
        functools.partial(late_kernel, cols, cycles, tiles),
        [(tile, 2 * tile // cols), covariance.shape],
        [
            first_even, first_odd, second_even, second_odd,
            panel, schur, near_panel, near_schur, held[-1], *partial, *schur_t,
        ],
        [vmem(half, tile), vmem(half, half)] + [vmem(*whole)] * 6 + [copies(8)],
        flops=4 * product,
    )
    return panels, trailing


def solution(mesh):
    rows, cols = mesh.shape["row"], mesh.shape["col"]

    def body(covariance, diag_inverse):
        return local(covariance, diag_inverse, rows, cols)

    return jax.shard_map(
        body,
        mesh=mesh,
        in_specs=(P("row", None, "col"), P()),
        out_specs=(P("row", "col"), P("row", None, "col")),
        check_vma=False,
    )
```

```python
import functools

import jax
import jax.numpy as jnp
from jax import lax
from jax.experimental import pallas as pl
from jax.experimental.pallas import tpu as pltpu
from jax.sharding import PartitionSpec as P

HIGHEST = lax.Precision.HIGHEST
AXES = ("row", "col")
SUB = 8


def dot(left, right, lhs_dim, rhs_dim):
    return lax.dot_general(
        left,
        right,
        (((lhs_dim,), (rhs_dim,)), ((), ())),
        precision=HIGHEST,
        preferred_element_type=jnp.float32,
    )


def nn(left, right):
    return dot(left, right, 1, 0)


def nt(left, right):
    return dot(left, right, 1, 1)


def tn(left, right):
    return dot(left, right, 0, 0)


def halves(value):
    high = value.astype(jnp.bfloat16)
    return high, (value - high.astype(jnp.float32)).astype(jnp.bfloat16)


def dot3(left, right, lhs_dim, rhs_dim):
    (a, b), (x, y) = halves(left), halves(right)

    def part(u, v):
        return lax.dot_general(
            u, v, (((lhs_dim,), (rhs_dim,)), ((), ())), preferred_element_type=jnp.float32
        )

    return part(a, x) + (part(a, y) + part(b, x))


def factor_block(work, aug):
    size = work.shape[0]
    groups = size // SUB
    rows = lax.broadcasted_iota(jnp.int32, (SUB, size), 0)
    lanes = lax.broadcasted_iota(jnp.int32, (SUB, size), 1)
    for t in range(groups):
        aug[t * SUB : (t + 1) * SUB, :] = jnp.where(lanes == rows + t * SUB, 1.0, 0.0)

    def lane(value, index):
        return jnp.broadcast_to(value[:, index : index + 1], (SUB, size))

    def row(value, index):
        return jnp.broadcast_to(value[index : index + 1, :], (SUB, size))

    for s in range(groups):
        here = slice(s * SUB, (s + 1) * SUB)
        own, own_aug = work[here, :], aug[here, :]
        columns = [lane(own, s * SUB + b) for b in range(SUB)]
        small = [[row(columns[b], a) if a >= b else None for b in range(SUB)] for a in range(SUB)]
        upper = [row(own, i) for i in range(SUB)]
        inverse = [row(own_aug, i) for i in range(SUB)]
        low = [[None] * SUB for _ in range(SUB)]
        scale = []
        for i in range(SUB):
            scale.append(lax.rsqrt(small[i][i]))
            for a in range(i + 1, SUB):
                low[a][i] = small[a][i] * scale[i]
            for b in range(i + 1, SUB):
                for a in range(b, SUB):
                    small[a][b] = small[a][b] - low[a][i] * low[b][i]
            upper[i] = upper[i] * scale[i]
            inverse[i] = inverse[i] * scale[i]
            for b in range(i + 1, SUB):
                upper[b] = upper[b] - upper[i] * low[b][i]
                inverse[b] = inverse[b] - inverse[i] * low[b][i]
        for t in range(s + 1, groups):
            there = slice(t * SUB, (t + 1) * SUB)
            current, current_aug = work[there, :], aug[there, :]
            part = [lane(current, s * SUB + b) for b in range(SUB)]
            for i in range(SUB):
                part[i] = part[i] * scale[i]
                for b in range(i + 1, SUB):
                    part[b] = part[b] - part[i] * low[b][i]
                current = current - part[i] * upper[i]
                current_aug = current_aug - part[i] * inverse[i]
            work[there, :] = current
            aug[there, :] = current_aug
        packed = inverse[0]
        for i in range(1, SUB):
            packed = jnp.where(rows == i, inverse[i], packed)
        aug[here, :] = packed


def masks(shape):
    return lax.broadcasted_iota(jnp.int32, shape, 0), lax.broadcasted_iota(jnp.int32, shape, 1)


def unpack(packed):
    half = packed.shape[1] // 2
    block = packed[:half, :half]
    rows, lanes = masks(block.shape)
    diag = jnp.broadcast_to(packed[half : half + 1, :half], block.shape)
    first = jnp.where(lanes <= rows, block, 0.0)
    second_t = jnp.where(lanes > rows, block, jnp.where(lanes == rows, diag, 0.0))
    return first, packed[:half, half:], second_t


def place():
    return lax.axis_index("row"), lax.axis_index("col")


def fetch(target, semaphore, choices):
    for condition, source in choices:

        @pl.when(condition)
        def _(source=source):
            pltpu.make_async_copy(source, target, semaphore).start()

    return pltpu.make_async_copy(choices[0][1], target, semaphore).wait


def call(kernel, out_shapes, inputs, scratch, vmem_inputs=0, flops=0):
    outs = [jax.ShapeDtypeStruct(shape, jnp.float32) for shape in out_shapes]
    size = sum(4 * x.size for x in inputs) + sum(4 * x.size for x in outs)
    return pl.pallas_call(
        kernel,
        out_shape=outs,
        in_specs=[
            pl.BlockSpec(memory_space=pltpu.VMEM if i < vmem_inputs else pl.ANY)
            for i in range(len(inputs))
        ],
        out_specs=[pl.BlockSpec(memory_space=pltpu.VMEM)] * len(outs),
        scratch_shapes=scratch,
        cost_estimate=pl.CostEstimate(flops=flops, bytes_accessed=size, transcendentals=0),
    )(*inputs)


def vmem(*shape):
    return pltpu.VMEM(shape, jnp.float32)


def copies(count):
    return pltpu.SemaphoreType.DMA((count,))


def split(refs, *counts):
    groups = []
    for count in counts:
        groups.append(refs[:count])
        refs = refs[count:]
    return groups


def extract_kernel(cov_ref, diag_ref, lead_ref, own_ref, low_ref, high_ref, *refs):
    held_refs, dinv, sems = refs[:-2], refs[-2], refs[-1]
    half = low_ref.shape[0]
    cycles = cov_ref.shape[1]
    r, c = place()
    source = (r == 0) & (c == 1)

    @pl.when(source)
    def _():
        pltpu.make_async_copy(diag_ref, dinv, sems.at[0]).start()

    own = cov_ref[:, 0, :]
    own_ref[...] = own
    low_ref[...] = own[:half]
    high_ref[...] = own[half:]
    for t, held_ref in enumerate(held_refs):
        later = cov_ref[:, min(t + 1, cycles - 1), :]
        held_ref[...] = jnp.where(c < 2, later, cov_ref[:, t, :])

    @pl.when(source)
    def _():
        pltpu.make_async_copy(diag_ref, dinv, sems.at[0]).wait()
        lead_ref[...] = nn(dinv[...], own_ref[...])

    @pl.when(jnp.logical_not(source))
    def _():
        lead_ref[...] = own_ref[...]


def factor_kernel(corner_ref, own_ref, out_ref, corner, second, diag, aug, first, last, cross, wide, sems):
    half = first.shape[0]
    part = half // 2
    r, c = place()
    owner = (r == 1) & (c == 1)
    a, b, low, high = slice(0, part), slice(part, half), slice(0, half), slice(half, 2 * half)

    @pl.when(owner)
    def _():
        waits = [
            fetch(corner, sems.at[0], [(owner, corner_ref)]),
            fetch(second, sems.at[1], [(owner, own_ref)]),
        ]
        for wait in waits:
            wait()
        second[...] = second[...] - tn(corner[...], corner[...])
        diag[...] = second[a, a]

        def upper_stage(inverse, base):
            inv = aug[...]
            inverse[a, a] = inv
            inverse[a, b] = jnp.zeros_like(inv)
            rows = slice(base, base + part)
            later = slice(base + part, base + half)
            cross[...] = nn(inv, second[rows, later])
            diag[...] = second[later, later] - tn(cross[...], cross[...])

        def lower_stage(inverse):
            inv = aug[...]
            inverse[b, b] = inv
            inverse[b, a] = -nn(inv, tn(cross[...], inverse[a, a]))

        def step(k, carry):
            factor_block(diag, aug)

            @pl.when(k == 0)
            def _():
                upper_stage(first, 0)

            @pl.when(k == 1)
            def _():
                lower_stage(first)
                wide[...] = nn(first[...], second[low, high])
                second[high, high] = second[high, high] - tn(wide[...], wide[...])
                diag[...] = second[half : half + part, half : half + part]

            @pl.when(k == 2)
            def _():
                upper_stage(last, half)

            @pl.when(k == 3)
            def _():
                lower_stage(last)

            return carry

        lax.fori_loop(0, 4, step, 0)
        inv = last[...]
        rows, lanes = masks(inv.shape)
        out_ref[:half, :half] = jnp.where(lanes <= rows, first[...], inv.T)
        out_ref[:half, half:] = -nn(inv, tn(wide[...], first[...]))
        diagonal = jnp.sum(jnp.where(lanes == rows, inv, 0.0), axis=0, keepdims=True)
        out_ref[half:, :half] = jnp.broadcast_to(diagonal, (SUB, half))
        out_ref[half:, half:] = jnp.zeros((SUB, half), jnp.float32)


def early_kernel(cols, cycles, tiles, *refs):
    hops = cols - 1
    (own, diag, near_held), low, high, mine, other, held, (panel_ref, near_ref), first_t, part, rest = split(
        refs, 3, hops, hops, tiles, tiles, tiles, 2, tiles, tiles, 4
    )
    first, dinv, column, sems = rest
    half = low[0].shape[0]
    r, c = place()
    core = r % 2
    always = c >= 0
    waits = [fetch(dinv, sems.at[0], [(always, diag)])]
    for i, parts in enumerate((low, high)):
        rows = pl.ds(i * half, half)
        choices = [(c == 0, own.at[rows])]
        choices += [(c == b, parts[b - 1]) for b in range(1, cols)]
        waits.append(fetch(first.at[rows], sems.at[1 + i], choices))
    for wait in waits:
        wait()
    panel_ref[...] = nt(first[...], dinv[...])
    for t in range(tiles):
        index = (t + jnp.where(c < 2, 1, 0)) * cols + c

        @pl.when(r >= index)
        def _(t=t):
            waits = [
                fetch(column, sems.at[3], [(core == 0, mine[t]), (core == 1, other[t])]),
                fetch(part[t], sems.at[4], [(always, held[t])]),
            ]
            for wait in waits:
                wait()
            first_t[t][...] = nn(dinv[...], column[...])
            part[t][...] = part[t][...] - nn(panel_ref[...], first_t[t][...])

    @pl.when((c >= 2) & (r == (cycles - 1) * cols + c))
    def _():
        fetch(near_ref, sems.at[4], [(always, near_held)])()
        near_ref[...] = near_ref[...] - nt(panel_ref[...], panel_ref[...])


def middle_kernel(cols, tiles, *refs):
    (even, odd, panel, own, back), low, high, mine, other, first_t, (pair_ref,), schur_t, rest = split(
        refs, 5, cols - 1, cols - 1, tiles, tiles, tiles, 1, tiles, 3
    )
    corner, column, sems = rest
    half = low[0].shape[0]
    r, c = place()
    core = r % 2
    always = c >= 0
    top, bottom = pl.ds(0, 2 * half), pl.ds(2 * half, 2 * half)
    waits = [
        fetch(corner, sems.at[0], [(core == 0, even), (core == 1, odd)]),
        fetch(pair_ref.at[top], sems.at[1], [(always, panel)]),
    ]
    for i, parts in enumerate((low, high)):
        rows = pl.ds(i * half, half)
        choices = [(c == 0, back.at[rows]), (c == 1, own.at[rows])]
        choices += [(c == b, parts[b - 2]) for b in range(2, cols)]
        waits.append(fetch(pair_ref.at[pl.ds((2 + i) * half, half)], sems.at[2 + i], choices))
    for wait in waits:
        wait()

    @pl.when(r == 1)
    def _():
        pair_ref[top, :] = corner[...].T

    pair_ref[bottom, :] = pair_ref[bottom, :] - nn(pair_ref[top, :], corner[...])
    for t in range(tiles):
        index = (t + jnp.where(c < 2, 1, 0)) * cols + c

        @pl.when(r >= index)
        def _(t=t):
            waits = [
                fetch(column, sems.at[4], [(always, first_t[t])]),
                fetch(schur_t[t], sems.at[5], [(core == 1, mine[t]), (core == 0, other[t])]),
            ]
            for wait in waits:
                wait()
            schur_t[t][...] = schur_t[t][...] - tn(corner[...], column[...])


def late_kernel(cols, cycles, tiles, *refs):
    (even, odd, pair, near_pair, held, near_part), first_part, schur_t, outs, rest = split(
        refs, 6, tiles, tiles, 2, 6
    )
    panels_ref, trailing_ref = outs
    packed, stack, other, column, total, sems = rest
    tile = total.shape[0]
    half = tile // 2
    low, high = slice(0, half), slice(half, tile)
    first, second = slice(0, tile), slice(tile, 2 * tile)
    r, c = place()
    core = r % 2
    always = c >= 0
    last = (cycles - 1) * cols + c
    own = (c >= 2) & (r == last)
    near = (c >= 2) & (r == last + 1) & (r // 2 == last // 2)
    waits = [
        fetch(packed, sems.at[0], [(core == 0, even), (core == 1, odd)]),
        fetch(stack, sems.at[1], [(always, pair)]),
    ]
    for wait in waits:
        wait()
    g_first, g_below, g_second_t = unpack(packed[...])

    def solve(target):
        left, right = target[second, low], target[second, high]
        target[second, low] = dot3(left, g_first, 1, 1)
        target[second, high] = dot3(left, g_below, 1, 1) + dot3(right, g_second_t, 1, 0)

    @pl.when(r == 0)
    def _():
        stack[second, :] = jnp.zeros((tile, tile), jnp.float32)

    @pl.when(r > 0)
    def _():
        solve(stack)

    width = panels_ref.shape[1]
    for b in range(cols):

        @pl.when(c == b)
        def _(b=b):
            rows, start = (first, b * width) if 2 * b < cols else (second, b * width - tile)
            panels_ref[...] = stack[rows, start : start + width]

    trailing_ref[...] = jnp.zeros_like(trailing_ref)

    def store(t):
        for shift in (0, 1):
            if t + shift < cycles:

                @pl.when((c < 2) if shift else (c >= 2))
                def _(slot=t + shift):
                    trailing_ref[:, slot, :] = total[...]

    for t in range(tiles):
        index = (t + jnp.where(c < 2, 1, 0)) * cols + c
        wanted = r >= index
        if t + 1 == cycles:
            wanted = wanted & jnp.logical_not(own | near)

        @pl.when(wanted)
        def _(t=t):
            waits = [
                fetch(column, sems.at[2], [(always, schur_t[t])]),
                fetch(total, sems.at[3], [(always, first_part[t])]),
            ]
            for wait in waits:
                wait()
            upper, lower = column[low], column[high]
            column[low] = dot3(g_first, upper, 1, 0)
            column[high] = dot3(g_below, upper, 1, 0) + dot3(g_second_t, lower, 0, 0)
            total[...] = total[...] - dot3(stack[second, :], column[...], 1, 0)
            store(t)

    @pl.when(own)
    def _():
        fetch(total, sems.at[3], [(always, near_part)])()
        other[second, :] = stack[second, :]

    @pl.when(near)
    def _():
        waits = [
            fetch(other, sems.at[2], [(always, near_pair)]),
            fetch(total, sems.at[3], [(always, held)]),
        ]
        for wait in waits:
            wait()
        solve(other)
        total[...] = total[...] - nt(stack[first, :], other[first, :])

    @pl.when(own | near)
    def _():
        total[...] = total[...] - dot3(stack[second, :], other[second, :], 1, 1)
        store(cycles - 1)


def local(covariance, diag_inverse, rows, cols):
    tile = covariance.shape[0]
    cycles = covariance.shape[1]
    half = tile // 2
    chips = rows // 2
    r, c = place()
    chip, core = r // 2, r % 2
    whole = (tile, tile)

    def send(value, pairs):
        flat = [(a * cols + b, x * cols + y) for (a, b), (x, y) in pairs]
        return lax.ppermute(value, AXES, flat)

    bits = []
    while (1 << len(bits)) < chips:
        bits.append(1 << len(bits))

    def column_of(t, column):
        return (t + (1 if column < 2 else 0)) * cols + column

    lead, own, own_low, own_high, *held = call(
        extract_kernel,
        [whole, whole, (half, tile), (half, tile)] + [whole] * cycles,
        [covariance, diag_inverse],
        [vmem(*whole), copies(1)],
        vmem_inputs=1,
    )

    swapped = send(lead, [((0, 1), (1, 1))])

    def along(column, hop):
        source = column - hop
        return [
            ((a, column), (a, column + 1))
            for a in range(rows)
            if (a >= 2 and source in (0, 1))
            or (a == 0 and source == 0 and hop == 0)
            or (a == 1 and source == 1)
        ]

    moved = []
    for part in (own_low, own_high):
        chain = []
        for hop in range(cols - 1):
            pairs = [pair for column in range(cols - 1) for pair in along(column, hop)]
            part = send(part, pairs)
            chain.append(part)
        moved.append(chain)
    back = send(lead, [((a, 1), (a, 0)) for a in range(rows) if a == 0 or a >= min(cols, rows - 1)])

    def spread(value, wanted, cores):
        current = value
        for step in range(len(bits)):
            pairs = []
            arrived = False
            for k in cores:
                order = bits if k == 0 else bits[::-1]
                used, bit, later = sum(order[:step]), order[step], sum(order[step + 1 :])
                arrived = jnp.where(core == k, (chip & bit) != 0, arrived)
                for column in range(cols):
                    for q in range(chips):
                        target = q | bit
                        if q & ~used or target >= chips:
                            continue
                        reach = {target | extra for extra in range(chips) if not extra & ~later}
                        if reach & wanted(column):
                            pairs.append(((2 * q + k, column), (2 * target + k, column)))
            if pairs:
                current = jnp.where(arrived, send(current, pairs), current)
        return current

    def trade(value, wanted, ways=(0, 1)):
        pairs = []
        for column in range(cols):
            for q in wanted(column):
                pairs += [((2 * q + k, column), (2 * q + 1 - k, column)) for k in ways]
        return send(value, pairs)

    mine, other = [], []
    for t in range(cycles):

        def wanted(column, t=t):
            if column < 2 and t + 1 >= cycles:
                return set()
            edge = column_of(t, column) // 2 + (1 if t + 1 == cycles else 0)
            return {q for q in range(chips) if q >= edge and q > 0}

        if any(wanted(column) for column in range(cols)):
            mine.append(spread(held[t], wanted, (0, 1)))
            other.append(trade(mine[-1], wanted))
    tiles = len(mine)

    part = half // 2
    packed = call(
        factor_kernel,
        [(half + SUB, tile)],
        [swapped, own],
        [vmem(*whole)] * 2
        + [vmem(part, part)] * 2
        + [vmem(half, half)] * 2
        + [vmem(part, part), vmem(half, half), copies(2)],
    )[0]

    def everyone(column):
        return set(range(chips))

    corner = jnp.where(c == 0, back, lead)
    for b in range(2, cols):
        corner = jnp.where(c == b, send(lead, [((0, 1), (0, b))]), corner)
    corner = spread(corner, everyone, (0,))
    corner_odd = trade(corner, everyone, (0,))

    piece = packed
    for b in range(cols):
        if b != 1:
            piece = jnp.where(c == b, send(packed, [((1, 1), (1, b))]), piece)
    piece_odd = spread(piece, everyone, (1,))
    piece_even = trade(piece_odd, everyone, (1,))

    product = 2 * tile**3
    panel, near_part, *products = call(
        functools.partial(early_kernel, cols, cycles, tiles),
        [whole] * (2 + 2 * tiles),
        [own, diag_inverse, held[-1], *moved[0], *moved[1], *mine, *other, *held[:tiles]],
        [vmem(*whole)] * 3 + [copies(5)],
        flops=3 * product,
    )
    first_t, partial = products[:tiles], products[tiles:]
    pair, *schur_t = call(
        functools.partial(middle_kernel, cols, tiles),
        [(2 * tile, tile)] + [whole] * tiles,
        [corner, corner_odd, panel, own, back, *moved[0], *moved[1], *mine, *other, *first_t],
        [vmem(*whole)] * 2 + [copies(6)],
        flops=2 * product,
    )
    edges = [column_of(cycles - 1, b) for b in range(2, cols)]
    pairs = [((j, b), (j + 1, b)) for b, j in zip(range(2, cols), edges) if j % 2 == 0]
    near_pair = send(pair, pairs)
    panels, trailing = call(
        functools.partial(late_kernel, cols, cycles, tiles),
        [(tile, 2 * tile // cols), covariance.shape],
        [piece_even, piece_odd, pair, near_pair, held[-1], near_part, *partial, *schur_t],
        [vmem(half + SUB, tile)] + [vmem(2 * tile, tile)] * 2 + [vmem(*whole)] * 2 + [copies(4)],
        flops=2 * product,
    )
    return panels, trailing


def solution(mesh):
    rows, cols = mesh.shape["row"], mesh.shape["col"]

    def body(covariance, diag_inverse):
        return local(covariance, diag_inverse, rows, cols)

    return jax.shard_map(
        body,
        mesh=mesh,
        in_specs=(P("row", None, "col"), P()),
        out_specs=(P("row", "col"), P("row", None, "col")),
        check_vma=False,
    )
```

```python
import functools

import jax
import jax.numpy as jnp
from jax import lax
from jax.experimental import pallas as pl
from jax.experimental.pallas import tpu as pltpu
from jax.sharding import PartitionSpec as P

HIGHEST = lax.Precision.HIGHEST
AXES = ("row", "col")
SUB = 8


def dot(left, right, lhs_dim, rhs_dim):
    return lax.dot_general(
        left,
        right,
        (((lhs_dim,), (rhs_dim,)), ((), ())),
        precision=HIGHEST,
        preferred_element_type=jnp.float32,
    )


def nn(left, right):
    return dot(left, right, 1, 0)


def nt(left, right):
    return dot(left, right, 1, 1)


def tn(left, right):
    return dot(left, right, 0, 0)


def halves(value):
    high = value.astype(jnp.bfloat16)
    return high, (value - high.astype(jnp.float32)).astype(jnp.bfloat16)


def dot3(left, right, lhs_dim, rhs_dim):
    (a, b), (x, y) = halves(left), halves(right)

    def part(u, v):
        return lax.dot_general(
            u, v, (((lhs_dim,), (rhs_dim,)), ((), ())), preferred_element_type=jnp.float32
        )

    return part(a, x) + (part(a, y) + part(b, x))


def factor_block(work, aug):
    size = work.shape[0]
    groups = size // SUB
    rows = lax.broadcasted_iota(jnp.int32, (SUB, size), 0)
    lanes = lax.broadcasted_iota(jnp.int32, (SUB, size), 1)
    for t in range(groups):
        aug[t * SUB : (t + 1) * SUB, :] = jnp.where(lanes == rows + t * SUB, 1.0, 0.0)

    def lane(value, index):
        return jnp.broadcast_to(value[:, index : index + 1], (SUB, size))

    def row(value, index):
        return jnp.broadcast_to(value[index : index + 1, :], (SUB, size))

    for s in range(groups):
        here = slice(s * SUB, (s + 1) * SUB)
        own, own_aug = work[here, :], aug[here, :]
        columns = [lane(own, s * SUB + b) for b in range(SUB)]
        small = [[row(columns[b], a) if a >= b else None for b in range(SUB)] for a in range(SUB)]
        upper = [row(own, i) for i in range(SUB)]
        inverse = [row(own_aug, i) for i in range(SUB)]
        low = [[None] * SUB for _ in range(SUB)]
        scale = []
        for i in range(SUB):
            scale.append(lax.rsqrt(small[i][i]))
            for a in range(i + 1, SUB):
                low[a][i] = small[a][i] * scale[i]
            for b in range(i + 1, SUB):
                for a in range(b, SUB):
                    small[a][b] = small[a][b] - low[a][i] * low[b][i]
            upper[i] = upper[i] * scale[i]
            inverse[i] = inverse[i] * scale[i]
            for b in range(i + 1, SUB):
                upper[b] = upper[b] - upper[i] * low[b][i]
                inverse[b] = inverse[b] - inverse[i] * low[b][i]
        for t in range(s + 1, groups):
            there = slice(t * SUB, (t + 1) * SUB)
            current, current_aug = work[there, :], aug[there, :]
            part = [lane(current, s * SUB + b) for b in range(SUB)]
            for i in range(SUB):
                part[i] = part[i] * scale[i]
                for b in range(i + 1, SUB):
                    part[b] = part[b] - part[i] * low[b][i]
                current = current - part[i] * upper[i]
                current_aug = current_aug - part[i] * inverse[i]
            work[there, :] = current
            aug[there, :] = current_aug
        packed = inverse[0]
        for i in range(1, SUB):
            packed = jnp.where(rows == i, inverse[i], packed)
        aug[here, :] = packed


def masks(shape):
    return lax.broadcasted_iota(jnp.int32, shape, 0), lax.broadcasted_iota(jnp.int32, shape, 1)


def unpack(packed):
    half = packed.shape[1] // 2
    block = packed[:half, :half]
    rows, lanes = masks(block.shape)
    diag = jnp.broadcast_to(packed[half : half + 1, :half], block.shape)
    first = jnp.where(lanes <= rows, block, 0.0)
    second_t = jnp.where(lanes > rows, block, jnp.where(lanes == rows, diag, 0.0))
    return first, packed[:half, half:], second_t


def place():
    return lax.axis_index("row"), lax.axis_index("col")


def fetch(target, semaphore, choices):
    for condition, source in choices:

        @pl.when(condition)
        def _(source=source):
            pltpu.make_async_copy(source, target, semaphore).start()

    return pltpu.make_async_copy(choices[0][1], target, semaphore).wait


def call(kernel, out_shapes, inputs, scratch, vmem_inputs=(), flops=0):
    outs = [jax.ShapeDtypeStruct(shape, jnp.float32) for shape in out_shapes]
    size = sum(4 * x.size for x in inputs) + sum(4 * x.size for x in outs)
    return pl.pallas_call(
        kernel,
        out_shape=outs,
        in_specs=[
            pl.BlockSpec(memory_space=pltpu.VMEM if i in vmem_inputs else pltpu.HBM)
            for i in range(len(inputs))
        ],
        out_specs=[pl.BlockSpec(memory_space=pltpu.VMEM)] * len(outs),
        scratch_shapes=scratch,
        cost_estimate=pl.CostEstimate(flops=flops, bytes_accessed=size, transcendentals=0),
    )(*inputs)


def vmem(*shape):
    return pltpu.VMEM(shape, jnp.float32)


def copies(count):
    return pltpu.SemaphoreType.DMA((count,))


def split(refs, *counts):
    groups = []
    for count in counts:
        groups.append(refs[:count])
        refs = refs[count:]
    return groups


def extract_kernel(cov_ref, diag_ref, lead_ref, low_ref, high_ref, *refs):
    held_refs, dinv, sems = refs[:-2], refs[-2], refs[-1]
    half = low_ref.shape[0]
    cycles = cov_ref.shape[1]
    r, c = place()
    source = (r == 0) & (c == 1)

    @pl.when(source)
    def _():
        pltpu.make_async_copy(diag_ref, dinv, sems.at[0]).start()

    own = cov_ref[:, 0, :]
    lead_ref[...] = own
    low_ref[...] = own[:half]
    high_ref[...] = own[half:]
    for t, held_ref in enumerate(held_refs):
        later = cov_ref[:, min(t + 1, cycles - 1), :]
        held_ref[...] = jnp.where(c < 2, later, cov_ref[:, t, :])

    @pl.when(source)
    def _():
        pltpu.make_async_copy(diag_ref, dinv, sems.at[0]).wait()
        lead_ref[...] = nn(dinv[...], lead_ref[...])


def factor_kernel(corner_ref, own_ref, out_ref, second, diag, aug, first, last, cross, wide, sems):
    half = first.shape[0]
    part = half // 2
    r, c = place()
    owner = (r == 1) & (c == 1)
    a, b, low, high = slice(0, part), slice(part, half), slice(0, half), slice(half, 2 * half)

    @pl.when(owner)
    def _():
        fetch(second, sems.at[0], [(owner, own_ref)])()
        second[...] = second[...] - tn(corner_ref[...], corner_ref[...])
        diag[...] = second[a, a]

        def upper_stage(inverse, base):
            inv = aug[...]
            inverse[a, a] = inv
            inverse[a, b] = jnp.zeros_like(inv)
            rows = slice(base, base + part)
            later = slice(base + part, base + half)
            cross[...] = nn(inv, second[rows, later])
            diag[...] = second[later, later] - tn(cross[...], cross[...])

        def lower_stage(inverse):
            inv = aug[...]
            inverse[b, b] = inv
            inverse[b, a] = -nn(inv, tn(cross[...], inverse[a, a]))

        def step(k, carry):
            factor_block(diag, aug)

            @pl.when(k == 0)
            def _():
                upper_stage(first, 0)

            @pl.when(k == 1)
            def _():
                lower_stage(first)
                wide[...] = nn(first[...], second[low, high])
                second[high, high] = second[high, high] - tn(wide[...], wide[...])
                diag[...] = second[half : half + part, half : half + part]

            @pl.when(k == 2)
            def _():
                upper_stage(last, half)

            @pl.when(k == 3)
            def _():
                lower_stage(last)

            return carry

        lax.fori_loop(0, 4, step, 0)
        inv = last[...]
        rows, lanes = masks(inv.shape)
        out_ref[:half, :half] = jnp.where(lanes <= rows, first[...], inv.T)
        out_ref[:half, half:] = -nn(inv, tn(wide[...], first[...]))
        diagonal = jnp.sum(jnp.where(lanes == rows, inv, 0.0), axis=0, keepdims=True)
        out_ref[half:, :half] = jnp.broadcast_to(diagonal, (SUB, half))
        out_ref[half:, half:] = jnp.zeros((SUB, half), jnp.float32)


def row_choices(cols, which, half, own, parts, back=None):
    _, c = place()
    rows = pl.ds(which * half, half)
    if back is None:
        return [(c == 0, own.at[rows])] + [(c == b, parts[b - 1]) for b in range(1, cols)]
    choices = [(c == 0, back.at[rows]), (c == 1, own.at[rows])]
    return choices + [(c == b, parts[b - 2]) for b in range(2, cols)]


def panel_kernel(cols, cycles, tiles, *refs):
    hops = cols - 1
    (own, back, diag, near_held), low, high, mine, other, held, (pair_ref, near_ref), first_t, part, rest = split(
        refs, 4, hops, hops - 1, tiles, tiles, tiles, 2, tiles, tiles, 2
    )
    dinv, sems = rest
    half = low[0].shape[0]
    r, c = place()
    core = r % 2
    always = c >= 0
    full = c < cols - 1
    top, bottom = slice(0, half), slice(half, 2 * half)
    waits = [
        fetch(dinv, sems.at[0], [(always, diag)]),
        fetch(pair_ref.at[top], sems.at[1], row_choices(cols, 0, half, own, low)),
        fetch(near_ref, sems.at[2], [(always, near_held)]),
    ]
    for i, parts in enumerate((low, high)):
        choices = row_choices(cols, i, half, own, parts, back)
        waits.append(fetch(pair_ref.at[pl.ds((2 + i) * half, half)], sems.at[3 + i], choices))
    for t in range(tiles):
        choices = [(core == 0, mine[t]), (core == 1, other[t])]
        waits.append(fetch(first_t[t], sems.at[6 + 2 * t], choices))
        waits.append(fetch(part[t], sems.at[7 + 2 * t], [(always, held[t])]))

    @pl.when(full)
    def _():
        fetch(pair_ref.at[bottom], sems.at[5], row_choices(cols - 1, 1, half, own, high))()

    for wait in waits:
        wait()

    def wanted(t):
        return r >= (t + jnp.where(c < 2, 1, 0)) * cols + c

    for t in range(tiles):

        @pl.when(wanted(t))
        def _(t=t):
            first_t[t][...] = nn(dinv[...], first_t[t][...])

    def rows_of(i, carry):
        rows = pl.ds(pl.multiple_of(i * half, half), half)
        pair_ref[rows, :] = nt(pair_ref[rows, :], dinv[...])
        for t in range(tiles):

            @pl.when(wanted(t))
            def _(t=t):
                part[t][rows, :] = part[t][rows, :] - nn(pair_ref[rows, :], first_t[t][...])

        return carry

    lax.fori_loop(0, jnp.where(full, 2, 1), rows_of, 0)

    @pl.when(full & (c >= 2) & (r == (cycles - 1) * cols + c))
    def _():
        tile = slice(0, 2 * half)
        near_ref[...] = near_ref[...] - nt(pair_ref[tile, :], pair_ref[tile, :])


def final_kernel(cols, cycles, tiles, *refs):
    (corner_odd, piece_even, corner_even, piece_odd, pair, near_pair, held, near_part, last_rows, diag), arrivals, first_t, mine, other, partial, outs, rest = split(
        refs, 10, cols // 2, tiles, tiles, tiles, tiles, 2, 8
    )
    panels_ref, trailing_ref = outs
    packed, corner, stacks, first, second, total, near_total, sems = rest
    stack, near_stack = stacks.at[0], stacks.at[1]
    tile = near_total.shape[0]
    half = tile // 2
    low, high = slice(0, half), slice(half, tile)
    top, bottom = slice(0, tile), slice(tile, 2 * tile)
    r, c = place()
    core = r % 2
    always = c >= 0
    last = (cycles - 1) * cols + c
    own = (c >= 2) & (r == last)
    near = (c >= 2) & (r == last + 1) & (r // 2 == last // 2)
    late = c == cols - 1

    def wanted(t):
        found = r >= (t + jnp.where(c < 2, 1, 0)) * cols + c
        return found & jnp.logical_not(own | near) if t + 1 == cycles else found

    mine_late = own & late

    @pl.when(near)
    def _():
        pltpu.make_async_copy(near_pair, near_stack, sems.at[1]).start()

    @pl.when(own | near)
    def _():
        fetch(near_total, sems.at[2], [(own & (c < cols - 1), near_part), (near | mine_late, held)])

    @pl.when(late)
    def _():
        pltpu.make_async_copy(diag, near_stack.at[top], sems.at[1]).start()
        pltpu.make_async_copy(pair.at[low], stack.at[low], sems.at[0]).start()
        pltpu.make_async_copy(pair.at[bottom], stack.at[bottom], sems.at[4]).start()
        pltpu.make_async_copy(last_rows, stack.at[high], sems.at[5]).start()

    @pl.when(jnp.logical_not(late))
    def _():
        pltpu.make_async_copy(pair, stack, sems.at[0]).start()

    waits = []
    for t in range(tiles):
        waits.append(fetch(first.at[t], sems.at[6 + 3 * t], [(always, first_t[t])]))
        choices = [(core == 1, mine[t]), (core == 0, other[t])]
        waits.append(fetch(second.at[t], sems.at[7 + 3 * t], choices))
        waits.append(fetch(total.at[t], sems.at[8 + 3 * t], [(always, partial[t])]))

    @pl.when(core == 0)
    def _():
        fetch(corner, sems.at[3], [(always, corner_even)])()
        packed[...] = piece_even[...]

    @pl.when(core == 1)
    def _():
        fetch(packed, sems.at[3], [(always, piece_odd)])()
        corner[...] = corner_odd[...]

    @pl.when(near)
    def _():
        pltpu.make_async_copy(near_pair, near_stack, sems.at[1]).wait()

    @pl.when(own | near)
    def _():
        pltpu.make_async_copy(held, near_total, sems.at[2]).wait()

    @pl.when(jnp.logical_not(late))
    def _():
        pltpu.make_async_copy(pair, stack, sems.at[0]).wait()

    for wait in waits:
        wait()

    @pl.when(late)
    def _():
        pltpu.make_async_copy(diag, near_stack.at[top], sems.at[1]).wait()
        pltpu.make_async_copy(pair.at[low], stack.at[low], sems.at[0]).wait()
        pltpu.make_async_copy(pair.at[bottom], stack.at[bottom], sems.at[4]).wait()
        pltpu.make_async_copy(last_rows, stack.at[high], sems.at[5]).wait()
        stack[high, :] = nt(stack[high, :], near_stack[top, :])
        for t in range(tiles):

            @pl.when(wanted(t))
            def _(t=t):
                total[t, high] = total[t, high] - nn(stack[high, :], first[t])

    @pl.when(r == 1)
    def _():
        stack[top, :] = corner[...].T
        for b, source in zip(range(cols // 2, cols), arrivals):

            @pl.when(c == b)
            def _(source=source):
                fetch(stack.at[bottom], sems.at[3], [(always, source)])()

    g_first, g_below, g_second_t = unpack(packed[...])

    def solve(i, carry):
        @pl.when((i == 0) | near)
        def _():
            target = stacks.at[i]
            target[bottom, :] = target[bottom, :] - nn(target[top, :], corner[...])
            left, right = target[bottom, low], target[bottom, high]
            target[bottom, low] = dot3(left, g_first, 1, 1)
            target[bottom, high] = dot3(left, g_below, 1, 1) + dot3(right, g_second_t, 1, 0)

        return carry

    lax.fori_loop(0, 2, solve, 0)

    @pl.when(r == 0)
    def _():
        stack[bottom, :] = jnp.zeros((tile, tile), jnp.float32)

    width = panels_ref.shape[1]
    for b in range(cols):

        @pl.when(c == b)
        def _(b=b):
            rows, start = (top, b * width) if 2 * b < cols else (bottom, b * width - tile)
            panels_ref[...] = stack[rows, start : start + width]

    trailing_ref[...] = jnp.zeros_like(trailing_ref)

    def store(t, value):
        for shift in (0, 1):
            if t + shift < cycles:

                @pl.when((c < 2) if shift else (c >= 2))
                def _(slot=t + shift):
                    trailing_ref[:, slot, :] = value

    for t in range(tiles):

        @pl.when(wanted(t))
        def _(t=t):
            second[t] = second[t] - tn(corner[...], first[t])
            upper, lower = second[t, low], second[t, high]
            second[t, low] = dot3(g_first, upper, 1, 0)
            second[t, high] = dot3(g_below, upper, 1, 0) + dot3(g_second_t, lower, 0, 0)
            store(t, total[t] - dot3(stack[bottom, :], second[t], 1, 0))

    @pl.when(own)
    def _():
        near_stack[...] = stack[...]

    @pl.when(near | (own & late))
    def _():
        near_total[...] = near_total[...] - nt(stack[top, :], near_stack[top, :])

    @pl.when(own | near)
    def _():
        store(cycles - 1, near_total[...] - dot3(stack[bottom, :], near_stack[bottom, :], 1, 1))


def local(covariance, diag_inverse, rows, cols):
    tile = covariance.shape[0]
    cycles = covariance.shape[1]
    half = tile // 2
    chips = rows // 2
    r, c = place()
    chip, core = r // 2, r % 2
    whole = (tile, tile)

    def send(value, pairs):
        flat = [(a * cols + b, x * cols + y) for (a, b), (x, y) in pairs]
        return lax.ppermute(value, AXES, flat)

    bits = []
    while (1 << len(bits)) < chips:
        bits.append(1 << len(bits))

    def column_of(t, column):
        return (t + (1 if column < 2 else 0)) * cols + column

    lead, own_low, own_high, *held = call(
        extract_kernel,
        [whole, (half, tile), (half, tile)] + [whole] * cycles,
        [covariance, diag_inverse],
        [vmem(*whole), copies(1)],
        vmem_inputs=(0,),
    )

    swapped = send(lead, [((0, 1), (1, 1))])

    def along(column, hop):
        source = column - hop
        return [
            ((a, column), (a, column + 1))
            for a in range(rows)
            if (a >= 2 and source in (0, 1)) or (a == 0 and source == 0 and hop == 0)
        ]

    moved = []
    for part in (own_low, own_high):
        chain = []
        for hop in range(cols - 1):
            pairs = [pair for column in range(cols - 1) for pair in along(column, hop)]
            part = send(part, pairs)
            chain.append(part)
        moved.append(chain)
    back = send(lead, [((a, 1), (a, 0)) for a in range(rows) if a == 0 or a >= min(cols, rows - 1)])

    def spread(value, wanted, cores, extra=()):
        current, arrivals = value, []
        for step in range(len(bits)):
            pairs = list(extra[step : step + 1])
            arrived = False
            for k in cores:
                order = bits if k == 0 else bits[::-1]
                used, bit, later = sum(order[:step]), order[step], sum(order[step + 1 :])
                arrived = jnp.where(core == k, (chip & bit) != 0, arrived)
                for column in range(cols):
                    for q in range(chips):
                        target = q | bit
                        if q & ~used or target >= chips:
                            continue
                        reach = {target | more for more in range(chips) if not more & ~later}
                        if reach & wanted(column):
                            pairs.append(((2 * q + k, column), (2 * target + k, column)))
            if pairs:
                arrivals.append(send(current, pairs))
                current = jnp.where(arrived, arrivals[-1], current)
        return current, arrivals

    def trade(value, wanted, ways=(0, 1)):
        pairs = []
        for column in range(cols):
            for q in wanted(column):
                pairs += [((2 * q + k, column), (2 * q + 1 - k, column)) for k in ways]
        return send(value, pairs)

    mine, other = [], []
    for t in range(cycles):

        def wanted(column, t=t):
            if column < 2 and t + 1 >= cycles:
                return set()
            edge = column_of(t, column) // 2 + (1 if t + 1 == cycles else 0)
            return {q for q in range(chips) if q >= edge and q > 0}

        if any(wanted(column) for column in range(cols)):
            mine.append(spread(held[t], wanted, (0, 1))[0])
            other.append(trade(mine[-1], wanted))
    tiles = len(mine)

    part = half // 2
    packed = call(
        factor_kernel,
        [(half + SUB, tile)],
        [swapped, lead],
        [vmem(*whole)]
        + [vmem(part, part)] * 2
        + [vmem(half, half)] * 2
        + [vmem(part, part), vmem(half, half), copies(1)],
        vmem_inputs=(0,),
    )[0]

    def everyone(column):
        return set(range(chips))

    corner, passed = jnp.where(c == 0, back, lead), lead
    for b in range(2, cols):
        passed = send(passed, [((0, b - 1), (0, b))])
        corner = jnp.where(c == b, passed, corner)
    extra = [((1, 1), (1, b)) for b in range(cols // 2, cols)]
    corner, arrivals = spread(corner, everyone, (0,), extra)
    corner_odd = trade(corner, everyone, (0,))

    piece = packed
    for b in range(cols):
        if b != 1:
            piece = jnp.where(c == b, send(packed, [((1, 1), (1, b))]), piece)
    piece_odd, _ = spread(piece, everyone, (1,))
    piece_even = trade(piece_odd, everyone, (1,))

    product = 2 * tile**3
    pair, near_part, *products = call(
        functools.partial(panel_kernel, cols, cycles, tiles),
        [(2 * tile, tile), whole] + [whole] * (2 * tiles),
        [
            lead, back, diag_inverse, held[-1],
            *moved[0], *moved[1][:-1], *mine, *other, *held[:tiles],
        ],
        [vmem(*whole), copies(6 + 2 * tiles)],
        flops=3 * product,
    )
    first_t, partial = products[:tiles], products[tiles:]
    edges = [column_of(cycles - 1, b) for b in range(2, cols)]
    pairs = [((j, b), (j + 1, b)) for b, j in zip(range(2, cols), edges) if j % 2 == 0]
    near_pair = send(pair, pairs)
    rows_of_one = cols // 2
    panels, trailing = call(
        functools.partial(final_kernel, cols, cycles, tiles),
        [(tile, 2 * tile // cols), covariance.shape],
        [
            corner_odd, piece_even, corner, piece_odd, pair, near_pair, held[-1], near_part,
            moved[1][-1], diag_inverse, *arrivals[:rows_of_one],
            *first_t, *mine, *other, *partial,
        ],
        [vmem(half + SUB, tile), vmem(*whole), vmem(2, 2 * tile, tile)]
        + [vmem(tiles, *whole)] * 3
        + [vmem(*whole), copies(6 + 3 * tiles)],
        vmem_inputs=(0, 1),
        flops=5 * product,
    )
    return panels, trailing


def solution(mesh):
    rows, cols = mesh.shape["row"], mesh.shape["col"]

    def body(covariance, diag_inverse):
        return local(covariance, diag_inverse, rows, cols)

    return jax.shard_map(
        body,
        mesh=mesh,
        in_specs=(P("row", None, "col"), P()),
        out_specs=(P("row", "col"), P("row", None, "col")),
        check_vma=False,
    )
```

```python
import functools

import jax
import jax.numpy as jnp
from jax import lax
from jax.experimental import pallas as pl
from jax.experimental.pallas import tpu as pltpu
from jax.sharding import PartitionSpec as P

HIGHEST = lax.Precision.HIGHEST
AXES = ("row", "col")
SUB = 8


def dot(left, right, lhs_dim, rhs_dim):
    return lax.dot_general(
        left,
        right,
        (((lhs_dim,), (rhs_dim,)), ((), ())),
        precision=HIGHEST,
        preferred_element_type=jnp.float32,
    )


def nn(left, right):
    return dot(left, right, 1, 0)


def nt(left, right):
    return dot(left, right, 1, 1)


def tn(left, right):
    return dot(left, right, 0, 0)


def halves(value):
    high = value.astype(jnp.bfloat16)
    return high, (value - high.astype(jnp.float32)).astype(jnp.bfloat16)


def dot3(left, right, lhs_dim, rhs_dim):
    (a, b), (x, y) = halves(left), halves(right)

    def part(u, v):
        return lax.dot_general(
            u, v, (((lhs_dim,), (rhs_dim,)), ((), ())), preferred_element_type=jnp.float32
        )

    return part(a, x) + (part(a, y) + part(b, x))


def factor_block(work, aug):
    size = work.shape[0]
    groups = size // SUB
    rows = lax.broadcasted_iota(jnp.int32, (SUB, size), 0)
    lanes = lax.broadcasted_iota(jnp.int32, (SUB, size), 1)
    for t in range(groups):
        aug[t * SUB : (t + 1) * SUB, :] = jnp.where(lanes == rows + t * SUB, 1.0, 0.0)

    def lane(value, index):
        return jnp.broadcast_to(value[:, index : index + 1], (SUB, size))

    def row(value, index):
        return jnp.broadcast_to(value[index : index + 1, :], (SUB, size))

    for s in range(groups):
        here = slice(s * SUB, (s + 1) * SUB)
        own, own_aug = work[here, :], aug[here, :]
        columns = [lane(own, s * SUB + b) for b in range(SUB)]
        small = [[row(columns[b], a) if a >= b else None for b in range(SUB)] for a in range(SUB)]
        upper = [row(own, i) for i in range(SUB)]
        inverse = [row(own_aug, i) for i in range(SUB)]
        low = [[None] * SUB for _ in range(SUB)]
        scale = []
        for i in range(SUB):
            scale.append(lax.rsqrt(small[i][i]))
            for a in range(i + 1, SUB):
                low[a][i] = small[a][i] * scale[i]
            for b in range(i + 1, SUB):
                for a in range(b, SUB):
                    small[a][b] = small[a][b] - low[a][i] * low[b][i]
            upper[i] = upper[i] * scale[i]
            inverse[i] = inverse[i] * scale[i]
            for b in range(i + 1, SUB):
                upper[b] = upper[b] - upper[i] * low[b][i]
                inverse[b] = inverse[b] - inverse[i] * low[b][i]
        for t in range(s + 1, groups):
            there = slice(t * SUB, (t + 1) * SUB)
            current, current_aug = work[there, :], aug[there, :]
            part = [lane(current, s * SUB + b) for b in range(SUB)]
            for i in range(SUB):
                part[i] = part[i] * scale[i]
                for b in range(i + 1, SUB):
                    part[b] = part[b] - part[i] * low[b][i]
                current = current - part[i] * upper[i]
                current_aug = current_aug - part[i] * inverse[i]
            work[there, :] = current
            aug[there, :] = current_aug
        packed = inverse[0]
        for i in range(1, SUB):
            packed = jnp.where(rows == i, inverse[i], packed)
        aug[here, :] = packed


def masks(shape):
    return lax.broadcasted_iota(jnp.int32, shape, 0), lax.broadcasted_iota(jnp.int32, shape, 1)


def unpack(packed):
    half = packed.shape[1] // 2
    block = packed[:half, :half]
    rows, lanes = masks(block.shape)
    diag = jnp.broadcast_to(packed[half : half + 1, :half], block.shape)
    first = jnp.where(lanes <= rows, block, 0.0)
    second_t = jnp.where(lanes > rows, block, jnp.where(lanes == rows, diag, 0.0))
    return first, packed[:half, half:], second_t


def place():
    return lax.axis_index("row"), lax.axis_index("col")


def fetch(target, semaphore, choices):
    for condition, source in choices:

        @pl.when(condition)
        def _(source=source):
            pltpu.make_async_copy(source, target, semaphore).start()

    return pltpu.make_async_copy(choices[0][1], target, semaphore).wait


def call(kernel, out_shapes, inputs, scratch, vmem_inputs=(), flops=0):
    outs = [jax.ShapeDtypeStruct(shape, jnp.float32) for shape in out_shapes]
    size = sum(4 * x.size for x in inputs) + sum(4 * x.size for x in outs)
    return pl.pallas_call(
        kernel,
        out_shape=outs,
        in_specs=[
            pl.BlockSpec(memory_space=pltpu.VMEM if i in vmem_inputs else pltpu.HBM)
            for i in range(len(inputs))
        ],
        out_specs=[pl.BlockSpec(memory_space=pltpu.VMEM)] * len(outs),
        scratch_shapes=scratch,
        cost_estimate=pl.CostEstimate(flops=flops, bytes_accessed=size, transcendentals=0),
    )(*inputs)


def vmem(*shape):
    return pltpu.VMEM(shape, jnp.float32)


def copies(count):
    return pltpu.SemaphoreType.DMA((count,))


def split(refs, *counts):
    groups = []
    for count in counts:
        groups.append(refs[:count])
        refs = refs[count:]
    return groups


def pick(choices, kept=None):
    count, shape = len(choices), choices[0][1].shape

    def kernel(*refs):
        out_ref, buffer, sems = refs[count:]
        r, c = place()
        for k, ((condition, _), source) in enumerate(zip(choices, refs[:count])):
            if k == kept:
                continue

            @pl.when(condition(r, c))
            def _(source=source):
                for i, (a, b) in enumerate(((source, buffer), (buffer, out_ref))):
                    copy = pltpu.make_async_copy(a, b, sems.at[i])
                    copy.start()
                    copy.wait()

    return pl.pallas_call(
        kernel,
        out_shape=jax.ShapeDtypeStruct(shape, jnp.float32),
        in_specs=[pl.BlockSpec(memory_space=pltpu.HBM)] * count,
        out_specs=pl.BlockSpec(memory_space=pltpu.HBM),
        scratch_shapes=[vmem(*shape), copies(2)],
        input_output_aliases={} if kept is None else {kept: 0},
    )(*[array for _, array in choices])


def extract_kernel(cov_ref, diag_ref, lead_ref, low_ref, high_ref, *refs):
    held_refs, dinv, sems = refs[:-2], refs[-2], refs[-1]
    half = low_ref.shape[0]
    cycles = cov_ref.shape[1]
    r, c = place()
    source = (r == 0) & (c == 1)

    @pl.when(source)
    def _():
        pltpu.make_async_copy(diag_ref, dinv, sems.at[0]).start()

    own = cov_ref[:, 0, :]
    lead_ref[...] = own
    low_ref[...] = own[:half]
    high_ref[...] = own[half:]
    for t, held_ref in enumerate(held_refs):
        later = cov_ref[:, min(t + 1, cycles - 1), :]
        held_ref[...] = jnp.where(c < 2, later, cov_ref[:, t, :])

    @pl.when(source)
    def _():
        pltpu.make_async_copy(diag_ref, dinv, sems.at[0]).wait()
        lead_ref[...] = nn(dinv[...], lead_ref[...])


def factor_kernel(corner_ref, own_ref, out_ref, second, diag, aug, first, last, cross, wide, sems):
    half = first.shape[0]
    part = half // 2
    r, c = place()
    owner = (r == 1) & (c == 1)
    a, b, low, high = slice(0, part), slice(part, half), slice(0, half), slice(half, 2 * half)

    @pl.when(owner)
    def _():
        fetch(second, sems.at[0], [(owner, own_ref)])()
        second[...] = second[...] - tn(corner_ref[...], corner_ref[...])
        diag[...] = second[a, a]

        def upper_stage(inverse, base):
            inv = aug[...]
            inverse[a, a] = inv
            inverse[a, b] = jnp.zeros_like(inv)
            rows = slice(base, base + part)
            later = slice(base + part, base + half)
            cross[...] = nn(inv, second[rows, later])
            diag[...] = second[later, later] - tn(cross[...], cross[...])

        def lower_stage(inverse):
            inv = aug[...]
            inverse[b, b] = inv
            inverse[b, a] = -nn(inv, tn(cross[...], inverse[a, a]))

        def step(k, carry):
            factor_block(diag, aug)

            @pl.when(k == 0)
            def _():
                upper_stage(first, 0)

            @pl.when(k == 1)
            def _():
                lower_stage(first)
                wide[...] = nn(first[...], second[low, high])
                second[high, high] = second[high, high] - tn(wide[...], wide[...])
                diag[...] = second[half : half + part, half : half + part]

            @pl.when(k == 2)
            def _():
                upper_stage(last, half)

            @pl.when(k == 3)
            def _():
                lower_stage(last)

            return carry

        lax.fori_loop(0, 4, step, 0)
        inv = last[...]
        rows, lanes = masks(inv.shape)
        out_ref[:half, :half] = jnp.where(lanes <= rows, first[...], inv.T)
        out_ref[:half, half:] = -nn(inv, tn(wide[...], first[...]))
        diagonal = jnp.sum(jnp.where(lanes == rows, inv, 0.0), axis=0, keepdims=True)
        out_ref[half:, :half] = jnp.broadcast_to(diagonal, (SUB, half))
        out_ref[half:, half:] = jnp.zeros((SUB, half), jnp.float32)


def row_choices(cols, which, half, own, parts, back=None):
    _, c = place()
    rows = pl.ds(which * half, half)
    if back is None:
        return [(c == 0, own.at[rows])] + [(c == b, parts[b - 1]) for b in range(1, cols)]
    choices = [(c == 0, back.at[rows]), (c == 1, own.at[rows])]
    return choices + [(c == b, parts[b - 2]) for b in range(2, cols)]


def panel_kernel(cols, cycles, tiles, *refs):
    hops = cols - 1
    (own, back, diag, near_held), low, high, mine, other, held, (pair_ref, near_ref), first_t, part, rest = split(
        refs, 4, hops, hops - 1, tiles, tiles, tiles, 2, tiles, tiles, 2
    )
    dinv, sems = rest
    half = low[0].shape[0]
    r, c = place()
    core = r % 2
    always = c >= 0
    full = c < cols - 1
    top, bottom = slice(0, half), slice(half, 2 * half)
    waits = [
        fetch(dinv, sems.at[0], [(always, diag)]),
        fetch(pair_ref.at[top], sems.at[1], row_choices(cols, 0, half, own, low)),
        fetch(near_ref, sems.at[2], [(always, near_held)]),
    ]
    for i, parts in enumerate((low, high)):
        choices = row_choices(cols, i, half, own, parts, back)
        waits.append(fetch(pair_ref.at[pl.ds((2 + i) * half, half)], sems.at[3 + i], choices))
    for t in range(tiles):
        choices = [(core == 0, mine[t]), (core == 1, other[t])]
        waits.append(fetch(first_t[t], sems.at[6 + 2 * t], choices))
        waits.append(fetch(part[t], sems.at[7 + 2 * t], [(always, held[t])]))

    @pl.when(full)
    def _():
        fetch(pair_ref.at[bottom], sems.at[5], row_choices(cols - 1, 1, half, own, high))()

    for wait in waits:
        wait()

    def wanted(t):
        return r >= (t + jnp.where(c < 2, 1, 0)) * cols + c

    for t in range(tiles):

        @pl.when(wanted(t))
        def _(t=t):
            first_t[t][...] = nn(dinv[...], first_t[t][...])

    def rows_of(i, carry):
        rows = pl.ds(pl.multiple_of(i * half, half), half)
        pair_ref[rows, :] = nt(pair_ref[rows, :], dinv[...])
        for t in range(tiles):

            @pl.when(wanted(t))
            def _(t=t):
                part[t][rows, :] = part[t][rows, :] - nn(pair_ref[rows, :], first_t[t][...])

        return carry

    lax.fori_loop(0, jnp.where(full, 2, 1), rows_of, 0)

    @pl.when(full & (c >= 2) & (r == (cycles - 1) * cols + c))
    def _():
        tile = slice(0, 2 * half)
        near_ref[...] = near_ref[...] - nt(pair_ref[tile, :], pair_ref[tile, :])


def final_kernel(cols, cycles, tiles, *refs):
    (corner_odd, piece_even, corner_even, piece_odd, pair, near_pair, held, near_part, last_rows, diag), arrivals, first_t, mine, other, partial, outs, rest = split(
        refs, 10, cols // 2, tiles, tiles, tiles, tiles, 2, 8
    )
    panels_ref, trailing_ref = outs
    packed, corner, stacks, first, second, total, near_total, sems = rest
    stack, near_stack = stacks.at[0], stacks.at[1]
    tile = near_total.shape[0]
    half = tile // 2
    low, high = slice(0, half), slice(half, tile)
    top, bottom = slice(0, tile), slice(tile, 2 * tile)
    r, c = place()
    core = r % 2
    always = c >= 0
    last = (cycles - 1) * cols + c
    own = (c >= 2) & (r == last)
    near = (c >= 2) & (r == last + 1) & (r // 2 == last // 2)
    late = c == cols - 1
    which = jnp.where(own, 0, 1)

    def wanted(t):
        found = r >= (t + jnp.where(c < 2, 1, 0)) * cols + c
        return found & jnp.logical_not(own | near) if t + 1 == cycles else found

    mine_late = own & late

    @pl.when(near)
    def _():
        pltpu.make_async_copy(near_pair, near_stack, sems.at[1]).start()

    @pl.when(own | near)
    def _():
        fetch(near_total, sems.at[2], [(own & (c < cols - 1), near_part), (near | mine_late, held)])

    @pl.when(late)
    def _():
        pltpu.make_async_copy(diag, near_stack.at[top], sems.at[1]).start()
        pltpu.make_async_copy(pair.at[low], stack.at[low], sems.at[0]).start()
        pltpu.make_async_copy(pair.at[bottom], stack.at[bottom], sems.at[4]).start()
        pltpu.make_async_copy(last_rows, stack.at[high], sems.at[5]).start()

    @pl.when(jnp.logical_not(late))
    def _():
        pltpu.make_async_copy(pair, stack, sems.at[0]).start()

    waits = []
    for t in range(tiles):
        waits.append(fetch(first.at[t], sems.at[6 + 3 * t], [(always, first_t[t])]))
        choices = [(core == 1, mine[t]), (core == 0, other[t])]
        waits.append(fetch(second.at[t], sems.at[7 + 3 * t], choices))
        waits.append(fetch(total.at[t], sems.at[8 + 3 * t], [(always, partial[t])]))

    @pl.when(core == 0)
    def _():
        fetch(corner, sems.at[3], [(always, corner_even)])()
        packed[...] = piece_even[...]

    @pl.when(core == 1)
    def _():
        fetch(packed, sems.at[3], [(always, piece_odd)])()
        corner[...] = corner_odd[...]

    @pl.when(near)
    def _():
        pltpu.make_async_copy(near_pair, near_stack, sems.at[1]).wait()

    @pl.when(jnp.logical_not(late))
    def _():
        pltpu.make_async_copy(pair, stack, sems.at[0]).wait()

    @pl.when(late)
    def _():
        pltpu.make_async_copy(diag, near_stack.at[top], sems.at[1]).wait()
        pltpu.make_async_copy(pair.at[low], stack.at[low], sems.at[0]).wait()
        pltpu.make_async_copy(pair.at[bottom], stack.at[bottom], sems.at[4]).wait()
        pltpu.make_async_copy(last_rows, stack.at[high], sems.at[5]).wait()
        stack[high, :] = nt(stack[high, :], near_stack[top, :])

    @pl.when(r == 1)
    def _():
        stack[top, :] = corner[...].T
        for b, source in zip(range(cols // 2, cols), arrivals):

            @pl.when(c == b)
            def _(source=source):
                fetch(stack.at[bottom], sems.at[3], [(always, source)])()

    g_first, g_below, g_second_t = unpack(packed[...])

    def solve(i, carry):
        @pl.when((i == 0) | near)
        def _():
            target = stacks.at[i]
            target[bottom, :] = target[bottom, :] - nn(target[top, :], corner[...])
            left, right = target[bottom, low], target[bottom, high]
            target[bottom, low] = dot3(left, g_first, 1, 1)
            target[bottom, high] = dot3(left, g_below, 1, 1) + dot3(right, g_second_t, 1, 0)

        return carry

    lax.fori_loop(0, 2, solve, 0)

    @pl.when(r == 0)
    def _():
        stack[bottom, :] = jnp.zeros((tile, tile), jnp.float32)

    width = panels_ref.shape[1]
    for b in range(cols):

        @pl.when(c == b)
        def _(b=b):
            rows, start = (top, b * width) if 2 * b < cols else (bottom, b * width - tile)
            panels_ref[...] = stack[rows, start : start + width]

    trailing_ref[...] = jnp.zeros_like(trailing_ref)
    for wait in waits:
        wait()

    def store(t, value):
        for shift in (0, 1):
            if t + shift < cycles:

                @pl.when((c < 2) if shift else (c >= 2))
                def _(slot=t + shift):
                    trailing_ref[:, slot, :] = value

    for t in range(tiles):

        @pl.when(wanted(t))
        def _(t=t):
            @pl.when(late)
            def _():
                total[t, high] = total[t, high] - nn(stack[high, :], first[t])

            second[t] = second[t] - tn(corner[...], first[t])
            upper, lower = second[t, low], second[t, high]
            second[t, low] = dot3(g_first, upper, 1, 0)
            second[t, high] = dot3(g_below, upper, 1, 0) + dot3(g_second_t, lower, 0, 0)
            store(t, total[t] - dot3(stack[bottom, :], second[t], 1, 0))

    @pl.when(own | near)
    def _():
        pltpu.make_async_copy(held, near_total, sems.at[2]).wait()

    @pl.when(near | (own & late))
    def _():
        near_total[...] = near_total[...] - nt(stack[top, :], stacks[which, top])

    @pl.when(own | near)
    def _():
        store(cycles - 1, near_total[...] - dot3(stack[bottom, :], stacks[which, bottom], 1, 1))


def local(covariance, diag_inverse, rows, cols):
    tile = covariance.shape[0]
    cycles = covariance.shape[1]
    half = tile // 2
    chips = rows // 2
    r, _ = place()
    chip, core = r // 2, r % 2
    whole = (tile, tile)

    def send(value, pairs):
        flat = [(a * cols + b, x * cols + y) for (a, b), (x, y) in pairs]
        return lax.ppermute(value, AXES, flat)

    bits = []
    while (1 << len(bits)) < chips:
        bits.append(1 << len(bits))

    def column_of(t, column):
        return (t + (1 if column < 2 else 0)) * cols + column

    lead, own_low, own_high, *held = call(
        extract_kernel,
        [whole, (half, tile), (half, tile)] + [whole] * cycles,
        [covariance, diag_inverse],
        [vmem(*whole), copies(1)],
        vmem_inputs=(0,),
    )

    swapped = send(lead, [((0, 1), (1, 1))])

    def along(column, hop):
        source = column - hop
        return [
            ((a, column), (a, column + 1))
            for a in range(rows)
            if (a >= 2 and source in (0, 1)) or (a == 0 and source == 0 and hop == 0)
        ]

    moved = []
    for part in (own_low, own_high):
        chain = []
        for hop in range(cols - 1):
            pairs = [pair for column in range(cols - 1) for pair in along(column, hop)]
            part = send(part, pairs)
            chain.append(part)
        moved.append(chain)
    back = send(lead, [((a, 1), (a, 0)) for a in range(rows) if a == 0 or a >= min(cols, rows - 1)])

    def spread(value, wanted, cores, kept=1):
        current = value
        for step in range(len(bits)):
            pairs, arrived, seen = [], False, {}
            for k in cores:
                order = bits if k == 0 else bits[::-1]
                used, bit, later = sum(order[:step]), order[step], sum(order[step + 1 :])
                arrived = jnp.where(core == k, (chip & bit) != 0, arrived)
                seen[k] = (used | bit, bit)
                for column in range(cols):
                    for q in range(chips):
                        target = q | bit
                        if q & ~used or target >= chips:
                            continue
                        reach = {target | more for more in range(chips) if not more & ~later}
                        if reach & wanted(column):
                            pairs.append(((2 * q + k, column), (2 * target + k, column)))
            if not pairs:
                continue
            got = send(current, pairs)
            if step + 1 == len(bits):
                current = jnp.where(arrived, got, current)
                continue

            def holds(r, c, new, seen=seen):
                found = False
                for k, (inside, bit) in seen.items():
                    at = (r % 2 == k) & ((r // 2 & ~inside) == 0)
                    found = found | (at & (((r // 2 & bit) != 0) == new))
                return found

            current = pick(
                [
                    (functools.partial(holds, new=True), got),
                    (functools.partial(holds, new=False), current),
                ],
                kept if step == 0 else 1,
            )
        return current

    def trade(value, wanted, ways=(0, 1)):
        pairs = []
        for column in range(cols):
            for q in wanted(column):
                pairs += [((2 * q + k, column), (2 * q + 1 - k, column)) for k in ways]
        return send(value, pairs)

    mine, other = [], []
    for t in range(cycles):

        def wanted(column, t=t):
            if column < 2 and t + 1 >= cycles:
                return set()
            edge = column_of(t, column) // 2 + (1 if t + 1 == cycles else 0)
            return {q for q in range(chips) if q >= edge and q > 0}

        if any(wanted(column) for column in range(cols)):
            mine.append(spread(held[t], wanted, (0, 1), kept=None))
            other.append(trade(mine[-1], wanted))
    tiles = len(mine)

    part = half // 2
    packed = call(
        factor_kernel,
        [(half + SUB, tile)],
        [swapped, lead],
        [vmem(*whole)]
        + [vmem(part, part)] * 2
        + [vmem(half, half)] * 2
        + [vmem(part, part), vmem(half, half), copies(1)],
        vmem_inputs=(0,),
    )[0]

    def everyone(column):
        return set(range(chips))

    choices = [
        (lambda r, c: (r == 0) & (c == 0), back),
        (lambda r, c: (r == 0) & (c == 1), lead),
    ]
    for b in range(2, cols):
        array = send(lead, [((0, 1), (0, b))])
        choices.append((lambda r, c, b=b: (r == 0) & (c == b), array))
    corner = pick(choices)
    corner = spread(corner, everyone, (0,))

    passed = []
    for b in range(cols // 2, cols):
        passed.append(send(lead, [((1, 1), (1, b))]))
    corner_odd = trade(corner, everyone, (0,))

    choices = [(lambda r, c: (r == 1) & (c == 1), packed)]
    for b in range(cols):
        if b != 1:
            array = send(packed, [((1, 1), (1, b))])
            choices.append((lambda r, c, b=b: (r == 1) & (c == b), array))
    piece = pick(choices, 0)
    piece_odd = spread(piece, everyone, (1,))
    piece_even = trade(piece_odd, everyone, (1,))

    product = 2 * tile**3
    pair, near_part, *products = call(
        functools.partial(panel_kernel, cols, cycles, tiles),
        [(2 * tile, tile), whole] + [whole] * (2 * tiles),
        [
            lead, back, diag_inverse, held[-1],
            *moved[0], *moved[1][:-1], *mine, *other, *held[:tiles],
        ],
        [vmem(*whole), copies(6 + 2 * tiles)],
        flops=3 * product,
    )
    first_t, partial = products[:tiles], products[tiles:]
    edges = [column_of(cycles - 1, b) for b in range(2, cols)]
    pairs = [((j, b), (j + 1, b)) for b, j in zip(range(2, cols), edges) if j % 2 == 0]
    near_pair = send(pair, pairs)
    panels, trailing = call(
        functools.partial(final_kernel, cols, cycles, tiles),
        [(tile, 2 * tile // cols), covariance.shape],
        [
            corner_odd, piece_even, corner, piece_odd, pair, near_pair, held[-1], near_part,
            moved[1][-1], diag_inverse, *passed,
            *first_t, *mine, *other, *partial,
        ],
        [vmem(half + SUB, tile), vmem(*whole), vmem(2, 2 * tile, tile)]
        + [vmem(tiles, *whole)] * 3
        + [vmem(*whole), copies(6 + 3 * tiles)],
        vmem_inputs=(0, 1),
        flops=5 * product,
    )
    return panels, trailing


def solution(mesh):
    rows, cols = mesh.shape["row"], mesh.shape["col"]

    def body(covariance, diag_inverse):
        return local(covariance, diag_inverse, rows, cols)

    return jax.shard_map(
        body,
        mesh=mesh,
        in_specs=(P("row", None, "col"), P()),
        out_specs=(P("row", "col"), P("row", None, "col")),
        check_vma=False,
    )
```

```python
import functools

import jax
import jax.numpy as jnp
from jax import lax
from jax.experimental import pallas as pl
from jax.experimental.pallas import tpu as pltpu
from jax.sharding import PartitionSpec as P

HIGHEST = lax.Precision.HIGHEST
AXES = ("row", "col")
SUB = 8


def dot(left, right, lhs_dim, rhs_dim):
    return lax.dot_general(
        left,
        right,
        (((lhs_dim,), (rhs_dim,)), ((), ())),
        precision=HIGHEST,
        preferred_element_type=jnp.float32,
    )


def nn(left, right):
    return dot(left, right, 1, 0)


def nt(left, right):
    return dot(left, right, 1, 1)


def tn(left, right):
    return dot(left, right, 0, 0)


def halves(value):
    high = value.astype(jnp.bfloat16)
    return high, (value - high.astype(jnp.float32)).astype(jnp.bfloat16)


def dot3(left, right, lhs_dim, rhs_dim):
    (a, b), (x, y) = halves(left), halves(right)

    def part(u, v):
        return lax.dot_general(
            u, v, (((lhs_dim,), (rhs_dim,)), ((), ())), preferred_element_type=jnp.float32
        )

    return part(a, x) + (part(a, y) + part(b, x))


def factor_block(work, aug):
    size = work.shape[0]
    groups = size // SUB
    rows = lax.broadcasted_iota(jnp.int32, (SUB, size), 0)
    lanes = lax.broadcasted_iota(jnp.int32, (SUB, size), 1)
    for t in range(groups):
        aug[t * SUB : (t + 1) * SUB, :] = jnp.where(lanes == rows + t * SUB, 1.0, 0.0)

    def lane(value, index):
        return jnp.broadcast_to(value[:, index : index + 1], (SUB, size))

    def row(value, index):
        return jnp.broadcast_to(value[index : index + 1, :], (SUB, size))

    for s in range(groups):
        here = slice(s * SUB, (s + 1) * SUB)
        own, own_aug = work[here, :], aug[here, :]
        columns = [lane(own, s * SUB + b) for b in range(SUB)]
        small = [[row(columns[b], a) if a >= b else None for b in range(SUB)] for a in range(SUB)]
        upper = [row(own, i) for i in range(SUB)]
        inverse = [row(own_aug, i) for i in range(SUB)]
        low = [[None] * SUB for _ in range(SUB)]
        scale = []
        for i in range(SUB):
            scale.append(lax.rsqrt(small[i][i]))
            for a in range(i + 1, SUB):
                low[a][i] = small[a][i] * scale[i]
            for b in range(i + 1, SUB):
                for a in range(b, SUB):
                    small[a][b] = small[a][b] - low[a][i] * low[b][i]
            upper[i] = upper[i] * scale[i]
            inverse[i] = inverse[i] * scale[i]
            for b in range(i + 1, SUB):
                upper[b] = upper[b] - upper[i] * low[b][i]
                inverse[b] = inverse[b] - inverse[i] * low[b][i]
        for t in range(s + 1, groups):
            there = slice(t * SUB, (t + 1) * SUB)
            current, current_aug = work[there, :], aug[there, :]
            part = [lane(current, s * SUB + b) for b in range(SUB)]
            for i in range(SUB):
                part[i] = part[i] * scale[i]
                for b in range(i + 1, SUB):
                    part[b] = part[b] - part[i] * low[b][i]
                current = current - part[i] * upper[i]
                current_aug = current_aug - part[i] * inverse[i]
            work[there, :] = current
            aug[there, :] = current_aug
        packed = inverse[0]
        for i in range(1, SUB):
            packed = jnp.where(rows == i, inverse[i], packed)
        aug[here, :] = packed


def masks(shape):
    return lax.broadcasted_iota(jnp.int32, shape, 0), lax.broadcasted_iota(jnp.int32, shape, 1)


def unpack(packed):
    half = packed.shape[1] // 2
    block = packed[:half, :half]
    rows, lanes = masks(block.shape)
    diag = jnp.broadcast_to(packed[half : half + 1, :half], block.shape)
    first = jnp.where(lanes <= rows, block, 0.0)
    second_t = jnp.where(lanes > rows, block, jnp.where(lanes == rows, diag, 0.0))
    return first, packed[:half, half:], second_t


def place():
    return lax.axis_index("row"), lax.axis_index("col")


def fetch(target, semaphore, choices):
    for condition, source in choices:

        @pl.when(condition)
        def _(source=source):
            pltpu.make_async_copy(source, target, semaphore).start()

    return pltpu.make_async_copy(choices[0][1], target, semaphore).wait


def call(kernel, out_shapes, inputs, scratch, vmem_inputs=(), flops=0):
    outs = [jax.ShapeDtypeStruct(shape, jnp.float32) for shape in out_shapes]
    size = sum(4 * x.size for x in inputs) + sum(4 * x.size for x in outs)
    return pl.pallas_call(
        kernel,
        out_shape=outs,
        in_specs=[
            pl.BlockSpec(memory_space=pltpu.VMEM if i in vmem_inputs else pltpu.HBM)
            for i in range(len(inputs))
        ],
        out_specs=[pl.BlockSpec(memory_space=pltpu.VMEM)] * len(outs),
        scratch_shapes=scratch,
        cost_estimate=pl.CostEstimate(flops=flops, bytes_accessed=size, transcendentals=0),
    )(*inputs)


def vmem(*shape):
    return pltpu.VMEM(shape, jnp.float32)


def copies(count):
    return pltpu.SemaphoreType.DMA((count,))


def split(refs, *counts):
    groups = []
    for count in counts:
        groups.append(refs[:count])
        refs = refs[count:]
    return groups


def pick(choices, kept=None):
    count, shape = len(choices), choices[0][1].shape

    def kernel(*refs):
        out_ref, buffer, sems = refs[count:]
        r, c = place()
        for k, ((condition, _), source) in enumerate(zip(choices, refs[:count])):
            if k == kept:
                continue

            @pl.when(condition(r, c))
            def _(source=source):
                for i, (a, b) in enumerate(((source, buffer), (buffer, out_ref))):
                    copy = pltpu.make_async_copy(a, b, sems.at[i])
                    copy.start()
                    copy.wait()

    return pl.pallas_call(
        kernel,
        out_shape=jax.ShapeDtypeStruct(shape, jnp.float32),
        in_specs=[pl.BlockSpec(memory_space=pltpu.HBM)] * count,
        out_specs=pl.BlockSpec(memory_space=pltpu.HBM),
        scratch_shapes=[vmem(*shape), copies(2)],
        input_output_aliases={} if kept is None else {kept: 0},
    )(*[array for _, array in choices])


def extract_kernel(cov_ref, diag_ref, lead_ref, low_ref, high_ref, *refs):
    held_refs, dinv, sems = refs[:-2], refs[-2], refs[-1]
    half = low_ref.shape[0]
    cycles = cov_ref.shape[1]
    r, c = place()
    source = (r == 0) & (c == 1)

    @pl.when(source)
    def _():
        pltpu.make_async_copy(diag_ref, dinv, sems.at[0]).start()

    own = cov_ref[:, 0, :]
    lead_ref[...] = own
    low_ref[...] = own[:half]
    high_ref[...] = own[half:]
    for t, held_ref in enumerate(held_refs):
        later = cov_ref[:, min(t + 1, cycles - 1), :]
        held_ref[...] = jnp.where(c < 2, later, cov_ref[:, t, :])

    @pl.when(source)
    def _():
        pltpu.make_async_copy(diag_ref, dinv, sems.at[0]).wait()
        lead_ref[...] = nn(dinv[...], lead_ref[...])


def factor_kernel(corner_ref, own_ref, out_ref, second, diag, aug, first, last, cross, wide, sems):
    half = first.shape[0]
    part = half // 2
    r, c = place()
    owner = (r == 1) & (c == 1)
    a, b, low, high = slice(0, part), slice(part, half), slice(0, half), slice(half, 2 * half)

    @pl.when(owner)
    def _():
        fetch(second, sems.at[0], [(owner, own_ref)])()
        second[...] = second[...] - tn(corner_ref[...], corner_ref[...])
        diag[...] = second[a, a]

        def upper_stage(inverse, base):
            inv = aug[...]
            inverse[a, a] = inv
            inverse[a, b] = jnp.zeros_like(inv)
            rows = slice(base, base + part)
            later = slice(base + part, base + half)
            cross[...] = nn(inv, second[rows, later])
            diag[...] = second[later, later] - tn(cross[...], cross[...])

        def lower_stage(inverse):
            inv = aug[...]
            inverse[b, b] = inv
            inverse[b, a] = -nn(inv, tn(cross[...], inverse[a, a]))

        def step(k, carry):
            factor_block(diag, aug)

            @pl.when(k == 0)
            def _():
                upper_stage(first, 0)

            @pl.when(k == 1)
            def _():
                lower_stage(first)
                wide[...] = nn(first[...], second[low, high])
                second[high, high] = second[high, high] - tn(wide[...], wide[...])
                diag[...] = second[half : half + part, half : half + part]

            @pl.when(k == 2)
            def _():
                upper_stage(last, half)

            @pl.when(k == 3)
            def _():
                lower_stage(last)

            return carry

        lax.fori_loop(0, 4, step, 0)
        inv = last[...]
        rows, lanes = masks(inv.shape)
        out_ref[:half, :half] = jnp.where(lanes <= rows, first[...], inv.T)
        out_ref[:half, half:] = -nn(inv, tn(wide[...], first[...]))
        diagonal = jnp.sum(jnp.where(lanes == rows, inv, 0.0), axis=0, keepdims=True)
        out_ref[half:, :half] = jnp.broadcast_to(diagonal, (SUB, half))
        out_ref[half:, half:] = jnp.zeros((SUB, half), jnp.float32)


def row_choices(cols, which, half, own, parts, back=None):
    _, c = place()
    rows = pl.ds(which * half, half)
    if back is None:
        return [(c == 0, own.at[rows])] + [(c == b, parts[b - 1]) for b in range(1, cols)]
    choices = [(c == 0, back.at[rows]), (c == 1, own.at[rows])]
    return choices + [(c == b, parts[b - 2]) for b in range(2, cols)]


def panel_kernel(cols, tiles, *refs):
    hops = cols - 1
    (own, back, diag), low, high, mine, other, held, (pair_ref,), first_t, part, rest = split(
        refs, 3, hops, hops - 1, tiles, tiles, tiles, 1, tiles, tiles, 2
    )
    dinv, sems = rest
    half = low[0].shape[0]
    r, c = place()
    core = r % 2
    always = c >= 0
    full = c < cols - 1
    top, bottom = slice(0, half), slice(half, 2 * half)
    waits = [
        fetch(dinv, sems.at[0], [(always, diag)]),
        fetch(pair_ref.at[top], sems.at[1], row_choices(cols, 0, half, own, low)),
    ]
    for i, parts in enumerate((low, high)):
        choices = row_choices(cols, i, half, own, parts, back)
        waits.append(fetch(pair_ref.at[pl.ds((2 + i) * half, half)], sems.at[3 + i], choices))
    for t in range(tiles):
        choices = [(core == 0, mine[t]), (core == 1, other[t])]
        waits.append(fetch(first_t[t], sems.at[6 + 2 * t], choices))
        waits.append(fetch(part[t], sems.at[7 + 2 * t], [(always, held[t])]))

    @pl.when(full)
    def _():
        fetch(pair_ref.at[bottom], sems.at[5], row_choices(cols - 1, 1, half, own, high))()

    for wait in waits:
        wait()

    def wanted(t):
        return r >= (t + jnp.where(c < 2, 1, 0)) * cols + c

    for t in range(tiles):

        @pl.when(wanted(t))
        def _(t=t):
            first_t[t][...] = nn(dinv[...], first_t[t][...])

    def rows_of(i, carry):
        rows = pl.ds(pl.multiple_of(i * half, half), half)
        pair_ref[rows, :] = nt(pair_ref[rows, :], dinv[...])
        for t in range(tiles):

            @pl.when(wanted(t))
            def _(t=t):
                part[t][rows, :] = part[t][rows, :] - nn(pair_ref[rows, :], first_t[t][...])

        return carry

    lax.fori_loop(0, jnp.where(full, 2, 1), rows_of, 0)


def final_kernel(cols, cycles, tiles, *refs):
    (corner_odd, piece_even, corner_even, piece_odd, pair, near_pair, held, last_rows, diag), arrivals, first_t, mine, other, partial, outs, rest = split(
        refs, 9, cols // 2, tiles, tiles, tiles, tiles, 2, 8
    )
    panels_ref, trailing_ref = outs
    packed, corner, stacks, first, second, total, near_total, sems = rest
    stack, near_stack = stacks.at[0], stacks.at[1]
    tile = near_total.shape[0]
    half = tile // 2
    low, high = slice(0, half), slice(half, tile)
    top, bottom = slice(0, tile), slice(tile, 2 * tile)
    r, c = place()
    core = r % 2
    always = c >= 0
    last = (cycles - 1) * cols + c
    own = (c >= 2) & (r == last)
    near = (c >= 2) & (r == last + 1) & (r // 2 == last // 2)
    late = c == cols - 1
    which = jnp.where(own, 0, 1)

    def wanted(t):
        found = r >= (t + jnp.where(c < 2, 1, 0)) * cols + c
        return found & jnp.logical_not(own | near) if t + 1 == cycles else found

    @pl.when(near)
    def _():
        pltpu.make_async_copy(near_pair, near_stack, sems.at[1]).start()

    @pl.when(own | near)
    def _():
        pltpu.make_async_copy(held, near_total, sems.at[2]).start()

    @pl.when(late)
    def _():
        pltpu.make_async_copy(diag, near_stack.at[top], sems.at[1]).start()
        pltpu.make_async_copy(pair.at[low], stack.at[low], sems.at[0]).start()
        pltpu.make_async_copy(pair.at[bottom], stack.at[bottom], sems.at[4]).start()
        pltpu.make_async_copy(last_rows, stack.at[high], sems.at[5]).start()

    @pl.when(jnp.logical_not(late))
    def _():
        pltpu.make_async_copy(pair, stack, sems.at[0]).start()

    waits = []
    for t in range(tiles):
        waits.append(fetch(first.at[t], sems.at[6 + 3 * t], [(always, first_t[t])]))
        choices = [(core == 1, mine[t]), (core == 0, other[t])]
        waits.append(fetch(second.at[t], sems.at[7 + 3 * t], choices))
        waits.append(fetch(total.at[t], sems.at[8 + 3 * t], [(always, partial[t])]))

    @pl.when(core == 0)
    def _():
        fetch(corner, sems.at[3], [(always, corner_even)])()
        packed[...] = piece_even[...]

    @pl.when(core == 1)
    def _():
        fetch(packed, sems.at[3], [(always, piece_odd)])()
        corner[...] = corner_odd[...]

    @pl.when(jnp.logical_not(late))
    def _():
        pltpu.make_async_copy(pair, stack, sems.at[0]).wait()

    @pl.when(late)
    def _():
        pltpu.make_async_copy(diag, near_stack.at[top], sems.at[1]).wait()
        pltpu.make_async_copy(pair.at[low], stack.at[low], sems.at[0]).wait()
        pltpu.make_async_copy(pair.at[bottom], stack.at[bottom], sems.at[4]).wait()
        pltpu.make_async_copy(last_rows, stack.at[high], sems.at[5]).wait()
        stack[high, :] = nt(stack[high, :], near_stack[top, :])

    @pl.when(r == 1)
    def _():
        stack[top, :] = corner[...].T
        for b, source in zip(range(cols // 2, cols), arrivals):

            @pl.when(c == b)
            def _(source=source):
                fetch(stack.at[bottom], sems.at[3], [(always, source)])()

    g_first, g_below, g_second_t = unpack(packed[...])

    def solve(i, carry):
        @pl.when((i == 1) & near)
        def _():
            pltpu.make_async_copy(near_pair, near_stack, sems.at[1]).wait()

        @pl.when((i == 0) | near)
        def _():
            target = stacks.at[i]
            target[bottom, :] = target[bottom, :] - nn(target[top, :], corner[...])
            left, right = target[bottom, low], target[bottom, high]
            target[bottom, low] = dot3(left, g_first, 1, 1)
            target[bottom, high] = dot3(left, g_below, 1, 1) + dot3(right, g_second_t, 1, 0)

        return carry

    lax.fori_loop(0, 2, solve, 0)

    @pl.when(r == 0)
    def _():
        stack[bottom, :] = jnp.zeros((tile, tile), jnp.float32)

    width = panels_ref.shape[1]
    for b in range(cols):

        @pl.when(c == b)
        def _(b=b):
            rows, start = (top, b * width) if 2 * b < cols else (bottom, b * width - tile)
            panels_ref[...] = stack[rows, start : start + width]

    @pl.when(jnp.logical_not(own | near))
    def _():
        trailing_ref[...] = jnp.zeros_like(trailing_ref)

    for wait in waits:
        wait()

    def store(t, value):
        for shift in (0, 1):
            if t + shift < cycles:

                @pl.when((c < 2) if shift else (c >= 2))
                def _(slot=t + shift):
                    trailing_ref[:, slot, :] = value

    for t in range(tiles):

        @pl.when(wanted(t))
        def _(t=t):
            @pl.when(late)
            def _():
                total[t, high] = total[t, high] - nn(stack[high, :], first[t])

            second[t] = second[t] - tn(corner[...], first[t])
            upper, lower = second[t, low], second[t, high]
            second[t, low] = dot3(g_first, upper, 1, 0)
            second[t, high] = dot3(g_below, upper, 1, 0) + dot3(g_second_t, lower, 0, 0)
            store(t, total[t] - dot3(stack[bottom, :], second[t], 1, 0))

    @pl.when(own | near)
    def _():
        pltpu.make_async_copy(held, near_total, sems.at[2]).wait()
        near_total[...] = near_total[...] - nt(stack[top, :], stacks[which, top])

    @pl.when(own | near)
    def _():
        store(cycles - 1, near_total[...] - dot3(stack[bottom, :], stacks[which, bottom], 1, 1))


def local(covariance, diag_inverse, rows, cols):
    tile = covariance.shape[0]
    cycles = covariance.shape[1]
    half = tile // 2
    chips = rows // 2
    r, _ = place()
    chip, core = r // 2, r % 2
    whole = (tile, tile)

    def send(value, pairs):
        flat = [(a * cols + b, x * cols + y) for (a, b), (x, y) in pairs]
        return lax.ppermute(value, AXES, flat)

    bits = []
    while (1 << len(bits)) < chips:
        bits.append(1 << len(bits))

    def column_of(t, column):
        return (t + (1 if column < 2 else 0)) * cols + column

    lead, own_low, own_high, *held = call(
        extract_kernel,
        [whole, (half, tile), (half, tile)] + [whole] * cycles,
        [covariance, diag_inverse],
        [vmem(*whole), copies(1)],
        vmem_inputs=(0,),
    )

    swapped = send(lead, [((0, 1), (1, 1))])

    def along(column, hop):
        source = column - hop
        return [
            ((a, column), (a, column + 1))
            for a in range(rows)
            if (a >= 2 and source in (0, 1)) or (a == 0 and source == 0 and hop == 0)
        ]

    moved = []
    for part in (own_low, own_high):
        chain = []
        for hop in range(cols - 1):
            pairs = [pair for column in range(cols - 1) for pair in along(column, hop)]
            part = send(part, pairs)
            chain.append(part)
        moved.append(chain)
    back = send(lead, [((a, 1), (a, 0)) for a in range(rows) if a == 0 or a >= min(cols, rows - 1)])

    def spread(value, wanted, cores, kept=1):
        current = value
        for step in range(len(bits)):
            pairs, arrived, seen = [], False, {}
            for k in cores:
                order = bits if k == 0 else bits[::-1]
                used, bit, later = sum(order[:step]), order[step], sum(order[step + 1 :])
                arrived = jnp.where(core == k, (chip & bit) != 0, arrived)
                seen[k] = (used | bit, bit)
                for column in range(cols):
                    for q in range(chips):
                        target = q | bit
                        if q & ~used or target >= chips:
                            continue
                        reach = {target | more for more in range(chips) if not more & ~later}
                        if reach & wanted(column):
                            pairs.append(((2 * q + k, column), (2 * target + k, column)))
            if not pairs:
                continue
            got = send(current, pairs)
            if step + 1 == len(bits):
                current = jnp.where(arrived, got, current)
                continue

            def holds(r, c, new, seen=seen):
                found = False
                for k, (inside, bit) in seen.items():
                    at = (r % 2 == k) & ((r // 2 & ~inside) == 0)
                    found = found | (at & (((r // 2 & bit) != 0) == new))
                return found

            current = pick(
                [
                    (functools.partial(holds, new=True), got),
                    (functools.partial(holds, new=False), current),
                ],
                kept if step == 0 else 1,
            )
        return current

    def trade(value, wanted, ways=(0, 1)):
        pairs = []
        for column in range(cols):
            for q in wanted(column):
                pairs += [((2 * q + k, column), (2 * q + 1 - k, column)) for k in ways]
        return send(value, pairs)

    mine, other = [], []
    for t in range(cycles):

        def wanted(column, t=t):
            if column < 2 and t + 1 >= cycles:
                return set()
            edge = column_of(t, column) // 2 + (1 if t + 1 == cycles else 0)
            return {q for q in range(chips) if q >= edge and q > 0}

        if any(wanted(column) for column in range(cols)):
            mine.append(spread(held[t], wanted, (0, 1), kept=None))
            other.append(trade(mine[-1], wanted))
    tiles = len(mine)

    part = half // 2
    packed = call(
        factor_kernel,
        [(half + SUB, tile)],
        [swapped, lead],
        [vmem(*whole)]
        + [vmem(part, part)] * 2
        + [vmem(half, half)] * 2
        + [vmem(part, part), vmem(half, half), copies(1)],
        vmem_inputs=(0,),
    )[0]

    def everyone(column):
        return set(range(chips))

    choices = [
        (lambda r, c: (r == 0) & (c == 0), back),
        (lambda r, c: (r == 0) & (c == 1), lead),
    ]
    for b in range(2, cols):
        array = send(lead, [((0, 1), (0, b))])
        choices.append((lambda r, c, b=b: (r == 0) & (c == b), array))
    corner = pick(choices)
    corner = spread(corner, everyone, (0,))

    passed = []
    for b in range(cols // 2, cols):
        passed.append(send(lead, [((1, 1), (1, b))]))
    corner_odd = trade(corner, everyone, (0,))

    choices = [(lambda r, c: (r == 1) & (c == 1), packed)]
    for b in range(cols):
        if b != 1:
            array = send(packed, [((1, 1), (1, b))])
            choices.append((lambda r, c, b=b: (r == 1) & (c == b), array))
    piece = pick(choices, 0)
    piece_odd = spread(piece, everyone, (1,))
    piece_even = trade(piece_odd, everyone, (1,))

    product = 2 * tile**3
    pair, *products = call(
        functools.partial(panel_kernel, cols, tiles),
        [(2 * tile, tile)] + [whole] * (2 * tiles),
        [
            lead, back, diag_inverse,
            *moved[0], *moved[1][:-1], *mine, *other, *held[:tiles],
        ],
        [vmem(*whole), copies(6 + 2 * tiles)],
        flops=3 * product,
    )
    first_t, partial = products[:tiles], products[tiles:]
    edges = [column_of(cycles - 1, b) for b in range(2, cols)]
    pairs = [((j, b), (j + 1, b)) for b, j in zip(range(2, cols), edges) if j % 2 == 0]
    near_pair = send(pair, pairs)
    panels, trailing = call(
        functools.partial(final_kernel, cols, cycles, tiles),
        [(tile, 2 * tile // cols), covariance.shape],
        [
            corner_odd, piece_even, corner, piece_odd, pair, near_pair, held[-1],
            moved[1][-1], diag_inverse, *passed,
            *first_t, *mine, *other, *partial,
        ],
        [vmem(half + SUB, tile), vmem(*whole), vmem(2, 2 * tile, tile)]
        + [vmem(tiles, *whole)] * 3
        + [vmem(*whole), copies(6 + 3 * tiles)],
        vmem_inputs=(0, 1),
        flops=5 * product,
    )
    return panels, trailing


def solution(mesh):
    rows, cols = mesh.shape["row"], mesh.shape["col"]

    def body(covariance, diag_inverse):
        return local(covariance, diag_inverse, rows, cols)

    return jax.shard_map(
        body,
        mesh=mesh,
        in_specs=(P("row", None, "col"), P()),
        out_specs=(P("row", "col"), P("row", None, "col")),
        check_vma=False,
    )
```
